256 devices in a mesh: section: 2 (over z_lo), tile: 128 (over y, z_hi, x, core).
Axes of the slice: x: 4, y: 4, z: 8 (z_hi: 4, z_lo: 2; z = z_hi * 2 + z_lo), core: 2. Of those that a mesh axis runs over, the one named last changes fastest.
Arguments:
- coarse: bfloat16 [12, 4096, 128], P(None, 'tile'), may hold values from -6 to 6
- lift_weight: bfloat16 [128, 12], replicated, may hold values from -1.75 to 1.75
- conv_weight: bfloat16 [3, 3, 128, 128], replicated, may hold values from -0.1875 to 0.1875
- out_weight: bfloat16 [4, 128], replicated, may hold values from -0.5 to 0.5
- denoise_in: bfloat16 [128, 8], replicated, may hold values from -2 to 2
- denoise_mid: bfloat16 [128, 128], replicated, may hold values from -0.5 to 0.5
- denoise_out: bfloat16 [4, 128], replicated, may hold values from -0.5 to 0.5
- base_noise: bfloat16 [4, 4, 4096, 128], P(None, None, 'tile'), may hold values from -5 to 5
- slot_noise: bfloat16 [4, 4, 4096, 128], P(None, None, 'tile'), may hold values from -5 to 5
- extra_dest: int32 [128, 8], P('tile'), may hold values from -1 to 127, as said below
Outputs:
- moments: float32 [2, 4, 4096, 128], P('section', None, 'tile')
The draws below stay inside these ranges and needn't reach their ends.
Inputs may be any that keep to these rules, and one draw needn't show every extreme that they name: `extra_dest`: the non-negative entries of row t come first and are consecutive device indices t + o, t + o + 1, ... (modulo 128) with 0 <= o and all of them within t to t + 8 - 1 modulo 128; the rest are -1. Every device is named exactly 4 times over all rows; some row has 8 non-negative entries.
All inputs are finite; a program needn't handle non-finite values.
Results may differ from the reference program's by a relative error of at most 0.0024.
Values may be sent and summed in bfloat16 or wider, within the bound.
A program may use at most 64 MiB of HBM per device.

```python
import math
import jax
import jax.numpy as jnp
from jax import lax

C = 128
CIN = 12
COUT = 4
TR = 32
TC = 128
MEMB = 4
XS = 4
NSTEP = 6
EMAX = 8
NT = 128
ROWS = 4096


def draw_extra_dest(key, part):
    first_key, second_key = jax.random.split(jax.random.fold_in(key, 11))
    rotation = jax.random.randint(first_key, (), 0, NT)
    shifts = jax.random.randint(second_key, (NT // 2,), 1 - XS, XS + 1)
    shifts = shifts.at[0].set(XS)
    tile_ids = jnp.arange(NT, dtype=jnp.int32)
    relative = jnp.mod(tile_ids - rotation, NT)
    pair_number = relative // 2
    leading = jnp.mod(relative, 2) == 0
    pair_start = jnp.mod(tile_ids - jnp.mod(relative, 2), NT)
    lead_count = XS + shifts[pair_number]
    member_count = jnp.where(leading, lead_count, XS - shifts[pair_number])
    member_ids = jnp.arange(EMAX, dtype=jnp.int32)
    local_slot = jnp.where(leading[:, None], member_ids[None, :], lead_count[:, None] + member_ids[None, :])
    target = jnp.mod(pair_start[:, None] + local_slot, NT)
    return jnp.where(member_ids[None, :] < member_count[:, None], target, -1).astype(jnp.int32)


def block_levels(stream_key, shape, pieces, low, high):
    factor_of = 1.0
    for axis_at, shards_of in pieces:
        draws = jax.random.uniform(jax.random.fold_in(jax.random.fold_in(stream_key, 6), axis_at), (shards_of,), jnp.float32, low / len(pieces), high / len(pieces))
        factor_of = factor_of * jnp.repeat(jnp.exp(draws), shape[axis_at] // shards_of).reshape((-1,) + (1,) * (len(shape) - 1 - axis_at))
    return factor_of


def normal_values(own_key, extent, width, reach, shards=(), kind=jnp.bfloat16):
    drawn = width * jax.random.normal(own_key, extent, jnp.float32)
    if shards:
        drawn = drawn * block_levels(own_key, extent, shards, -0.22, 0.18)
    return jnp.clip(drawn, -reach, reach).astype(kind)


def setup_inputs(seed: int = 0) -> dict:
    arg_keys = jax.random.split(jax.random.key(seed), 11)
    coarse = normal_values(arg_keys[0], (CIN, ROWS, TC), 1.0, 6.0, ((1, 128),))
    lift_weight = normal_values(arg_keys[1], (C, CIN), CIN ** -0.5, 1.75)
    conv_weight = normal_values(arg_keys[2], (3, 3, C, C), (9 * C) ** -0.5, 0.1875)
    out_weight = normal_values(arg_keys[3], (COUT, C), C ** -0.5, 0.5)
    denoise_in = normal_values(arg_keys[4], (C, 2 * COUT), (2 * COUT) ** -0.5, 2.0)
    denoise_mid = normal_values(arg_keys[5], (C, C), C ** -0.5, 0.5)
    denoise_out = normal_values(arg_keys[6], (COUT, C), C ** -0.5, 0.5)
    base_noise = normal_values(arg_keys[7], (MEMB, COUT, ROWS, TC), 1.0, 5.0, ((2, 128),))
    slot_noise = normal_values(arg_keys[8], (XS, COUT, ROWS, TC), 1.0, 5.0, ((2, 128),))
    extra_dest = draw_extra_dest(jax.random.fold_in(arg_keys[10], 71), 0)
    return {"coarse": coarse, "lift_weight": lift_weight, "conv_weight": conv_weight, "out_weight": out_weight, "denoise_in": denoise_in, "denoise_mid": denoise_mid, "denoise_out": denoise_out, "base_noise": base_noise, "slot_noise": slot_noise, "extra_dest": extra_dest}


SIGMA_MAX = 4.0
SIGMA_MIN = 0.25
PLAN_POWER = 7.0

def sigma_table(step_count):
    upper_root = SIGMA_MAX ** (1.0 / PLAN_POWER)
    lower_root = SIGMA_MIN ** (1.0 / PLAN_POWER)
    values = []
    for position in range(step_count):
        fraction = position / (step_count - 1)
        values.append((upper_root + fraction * (lower_root - upper_root)) ** PLAN_POWER)
    values.append(0.0)
    return values

def slot_sources(routes, device, slot_count):
    tile_count = routes.shape[0]
    named_here = jnp.any(routes == device, axis=1).astype(jnp.int32)
    before = (jnp.cumsum(named_here) - named_here).astype(jnp.int32)
    wanted = (before[None, :] == jnp.arange(slot_count, dtype=jnp.int32)[:, None]) & (named_here[None, :] == 1)
    tile_ids = jnp.arange(tile_count, dtype=jnp.int32)
    sources = lax.optimization_barrier(jnp.sum(jnp.where(wanted, tile_ids[None, :], 0), axis=1)).astype(jnp.int32)
    return (sources, jnp.any(wanted, axis=1))

def regress(window, lift_weight, conv_weight, out_weight):
    channels_in, height, width_cells = window.shape
    lifted = jnp.dot(lift_weight, window.reshape(channels_in, height * width_cells), preferred_element_type=jnp.float32)
    lifted = jax.nn.silu(lifted).astype(jnp.bfloat16).reshape(1, -1, height, width_cells)
    convolved = lax.conv_general_dilated(lifted.astype(jnp.float32), conv_weight.astype(jnp.float32), (1, 1), ((0, 0), (1, 1)), dimension_numbers=('NCHW', 'HWIO', 'NCHW'))
    features = jax.nn.silu(convolved[0]).astype(jnp.bfloat16)
    rows_out = height - 2
    produced = jnp.dot(out_weight, features.reshape(-1, rows_out * width_cells), preferred_element_type=jnp.float32)
    return produced.astype(jnp.bfloat16).reshape(-1, rows_out, width_cells)

def network(scaled, condition, denoise_in, denoise_mid, denoise_out):
    stacked = jnp.concatenate([scaled, condition], axis=1).astype(jnp.float32)
    first_hidden = jax.nn.silu(jnp.einsum('ci,kirw->kcrw', denoise_in.astype(jnp.float32), stacked)).astype(jnp.bfloat16)
    second_hidden = jax.nn.silu(jnp.einsum('cd,kdrw->kcrw', denoise_mid.astype(jnp.float32), first_hidden.astype(jnp.float32))).astype(jnp.bfloat16)
    return jnp.einsum('oc,kcrw->korw', denoise_out.astype(jnp.float32), second_hidden.astype(jnp.float32))

def denoise(condition, noise, denoise_in, denoise_mid, denoise_out):
    sigmas = sigma_table(NSTEP)
    latent = sigmas[0] * noise.astype(jnp.float32)
    for position in range(NSTEP):
        sigma_now = sigmas[position]
        sigma_next = sigmas[position + 1]
        input_scale = 1.0 / math.sqrt(sigma_now * sigma_now + 1.0)
        skip_scale = 1.0 / (sigma_now * sigma_now + 1.0)
        output_scale = sigma_now * input_scale
        scaled = (input_scale * latent).astype(jnp.bfloat16)
        denoised = skip_scale * latent + output_scale * network(scaled, condition, denoise_in, denoise_mid, denoise_out)
        latent = latent + (sigma_next - sigma_now) / sigma_now * (latent - denoised)
    return condition.astype(jnp.float32) + latent

def reference(coarse, lift_weight, conv_weight, out_weight, denoise_in, denoise_mid, denoise_out, base_noise, slot_noise, extra_dest):
    padded = jnp.pad(coarse, ((0, 0), (1, 1), (0, 0)))

    def regress_tile(tile_number):
        window = lax.dynamic_slice_in_dim(padded, tile_number * TR, TR + 2, 1)
        return regress(window, lift_weight, conv_weight, out_weight)
    tile_ids = jnp.arange(NT, dtype=jnp.int32)
    produced = lax.map(regress_tile, tile_ids)
    base_tiles = jnp.transpose(base_noise.reshape(MEMB, COUT, NT, TR, TC), (2, 0, 1, 3, 4))

    def base_members(inputs):
        condition, noises = inputs
        samples = denoise(jnp.broadcast_to(condition[None], noises.shape), noises, denoise_in, denoise_mid, denoise_out)
        return (lax.optimization_barrier(jnp.sum(samples, axis=0)), lax.optimization_barrier(jnp.sum(samples * samples, axis=0)))
    base_sum, base_square = lax.map(base_members, (produced, base_tiles))
    slot_tiles = jnp.transpose(slot_noise.reshape(XS, COUT, NT, TR, TC), (2, 0, 1, 3, 4))

    def slot_members(inputs):
        device, noises = inputs
        sources, slot_live = slot_sources(extra_dest, device, XS)
        samples = denoise(produced[sources], noises, denoise_in, denoise_mid, denoise_out)
        samples = jnp.where(slot_live[:, None, None, None], samples, 0.0)
        return (samples, sources)
    slot_samples, slot_from = lax.map(slot_members, (tile_ids, slot_tiles))
    flat_samples = slot_samples.reshape(NT * XS, COUT, TR, TC)
    flat_from = slot_from.reshape(NT * XS)
    extra_sum = jax.ops.segment_sum(flat_samples, flat_from, num_segments=NT)
    extra_square = jax.ops.segment_sum(flat_samples * flat_samples, flat_from, num_segments=NT)
    member_count = (MEMB + lax.optimization_barrier(jnp.sum((extra_dest >= 0).astype(jnp.int32), axis=1))).astype(jnp.float32)
    scale_back = member_count[:, None, None, None]
    ensemble_mean = (base_sum + extra_sum) / scale_back
    ensemble_var = (base_square + extra_square) / scale_back - ensemble_mean * ensemble_mean
    moments = jnp.stack([ensemble_mean, ensemble_var])
    return jnp.transpose(moments, (0, 2, 1, 3, 4)).reshape(2, COUT, NT * TR, TC)
```

```python
import functools
import math

import jax
import jax.numpy as jnp
from jax import lax
from jax.experimental import pallas as pl
from jax.experimental.pallas import tpu as pltpu
from jax.sharding import PartitionSpec as P

MESH = pl.DeviceIdType.MESH
BF = jnp.bfloat16
F32 = jnp.float32
MEMB = 4
SLOTS = 4
NSTEP = 6
REACH = 8
SIGMA_MAX = 4.0
SIGMA_MIN = 0.25
PLAN_POWER = 7.0


def sigma_table(step_count):
    upper_root = SIGMA_MAX ** (1.0 / PLAN_POWER)
    lower_root = SIGMA_MIN ** (1.0 / PLAN_POWER)
    values = []
    for position in range(step_count):
        fraction = position / (step_count - 1)
        values.append((upper_root + fraction * (lower_root - upper_root)) ** PLAN_POWER)
    values.append(0.0)
    return values


SIGMAS = sigma_table(NSTEP)


def step_factors():
    table = []
    for position in range(NSTEP):
        now, later = SIGMAS[position], SIGMAS[position + 1]
        scale = 1.0 / math.sqrt(now * now + 1.0)
        slope = (later - now) / now
        table.append((scale, 1.0 + slope * (1.0 - scale * scale), -slope * now * scale))
    return table


FACTORS = step_factors()


def pick(position, column):
    value = jnp.float32(FACTORS[NSTEP - 1][column])
    for step in range(NSTEP - 2, -1, -1):
        value = jnp.where(position == step, jnp.float32(FACTORS[step][column]), value)
    return value


def silu_of_half(half):
    return (half + half * jnp.tanh(half)).astype(BF)


def spread(rows, columns, by_row, group):
    i = lax.broadcasted_iota(jnp.int32, (rows, columns), 0)
    j = lax.broadcasted_iota(jnp.int32, (rows, columns), 1)
    same = (i // group == j) if by_row else (j // group == i)
    return same.astype(F32).astype(BF)


def kernel(
    tiles,
    coarse_ref,
    lift_ref,
    conv_ref,
    outw_ref,
    din_ref,
    dmid_ref,
    dout_ref,
    base_ref,
    slot_ref,
    dest_ref,
    out_ref,
    cv,
    wraw,
    noise,
    halo_out,
    halo_in,
    lifted,
    wconv,
    feat,
    fout,
    ein,
    emid,
    eout,
    hid1,
    hid2,
    lat,
    cond,
    gx,
    piece,
    arrived,
    swap_out,
    swap_in,
    local_sem,
    send_sem,
    recv_sem,
):
    section = lax.axis_index("section")
    tile = lax.axis_index("tile")
    half_rows = out_ref.shape[2] // 2
    cells = out_ref.shape[3]
    channels = din_ref.shape[0]
    fields = out_ref.shape[1]
    flat = fields * half_rows
    cin = lift_ref.shape[1]
    octet = half_rows // 2
    first = pl.multiple_of(section * half_rows, half_rows)

    copies = [
        pltpu.make_async_copy(coarse_ref, cv, local_sem.at[0]),
        pltpu.make_async_copy(conv_ref, wraw, local_sem.at[1]),
        pltpu.make_async_copy(
            base_ref.at[:, :, pl.ds(first, half_rows), :], noise.at[0], local_sem.at[2]
        ),
        pltpu.make_async_copy(
            slot_ref.at[:, :, pl.ds(first, half_rows), :], noise.at[1], local_sem.at[3]
        ),
    ]
    for copy in copies:
        copy.start()

    ahead = [lax.rem(tile + o, tiles) for o in range(REACH)]
    behind = [lax.rem(tile + tiles - o, tiles) for o in range(REACH)]

    barrier = pltpu.get_barrier_semaphore()
    for o in range(1, REACH):
        for other in (ahead[o], behind[o]):
            pl.semaphore_signal(barrier, inc=1, device_id={"tile": other}, device_id_type=MESH)
    pl.semaphore_signal(
        barrier, inc=1, device_id={"section": 1 - section}, device_id_type=MESH
    )

    copies[0].wait()
    top_half = section == 0
    last_row = cv[:, 2 * half_rows - 1, :].astype(F32)
    first_row = cv[:, 0, :].astype(F32)
    halo_out[...] = jnp.zeros(halo_out.shape, BF)
    halo_out[0:cin, :] = jnp.where(top_half, last_row, first_row).astype(BF)

    pl.semaphore_wait(barrier, 2 * (REACH - 1) + 1)
    halo_target = lax.rem(jnp.where(top_half, tile + 1, tile + tiles - 1), tiles)
    halo_copy = pltpu.make_async_remote_copy(
        src_ref=halo_out,
        dst_ref=halo_in,
        send_sem=send_sem.at[0],
        recv_sem=recv_sem.at[0],
        device_id={"tile": halo_target},
        device_id_type=MESH,
    )
    halo_copy.start()

    lift_half = lift_ref[...].astype(F32) * 0.5
    lift_bf = lift_half.astype(BF)
    wide = jnp.dot(lift_bf, spread(cin, cin * octet, False, octet), preferred_element_type=F32)
    lane = lax.broadcasted_iota(jnp.int32, wide.shape, 1) % octet
    own = cv[:, pl.ds(first, half_rows), :].astype(F32)
    own = jnp.concatenate(
        [
            own[:, :octet, :].reshape(cin * octet, cells),
            own[:, octet:, :].reshape(cin * octet, cells),
        ],
        axis=1,
    ).astype(BF)
    for r in range(octet):
        weight = jnp.where(lane == r, wide, 0.0).astype(BF)
        lifted[(r + 1) * channels : (r + 2) * channels, :] = silu_of_half(
            jnp.dot(weight, own, preferred_element_type=F32)
        )
    copies[1].wait()
    for a in range(3):
        for b in range(3):
            wconv[b * channels : (b + 1) * channels, a * channels : (a + 1) * channels] = (
                (wraw[a, b].astype(F32) * 0.5).T.astype(BF)
            )
    wide_in = (
        jnp.dot(
            din_ref[...], spread(2 * fields, 2 * flat, False, half_rows), preferred_element_type=F32
        )
        * 0.5
    )
    lane_in = lax.broadcasted_iota(jnp.int32, wide_in.shape, 1) % half_rows
    wide_out = jnp.dot(
        spread(flat, fields, True, half_rows), dout_ref[...], preferred_element_type=F32
    )
    row_out = lax.broadcasted_iota(jnp.int32, wide_out.shape, 0) % half_rows
    for r in range(half_rows):
        block = slice(r * channels, (r + 1) * channels)
        ein[block, :] = jnp.where(lane_in == r, wide_in, 0.0).astype(BF)
        eout[:, block] = jnp.where(row_out == r, wide_out, 0.0).astype(BF)
    mid = (dmid_ref[...].astype(F32) * 0.5).astype(BF)
    emid[...] = jnp.zeros(emid.shape, BF)
    emid[:channels, :channels] = mid
    emid[channels:, channels:] = mid
    wide_reg = jnp.dot(
        spread(fields * octet, fields, True, octet), outw_ref[...], preferred_element_type=F32
    )
    row_reg = lax.broadcasted_iota(jnp.int32, wide_reg.shape, 0) % octet
    for r in range(octet):
        fout[:, r * channels : (r + 1) * channels] = jnp.where(row_reg == r, wide_reg, 0.0).astype(
            BF
        )
    for k in range(2):
        copies[2 + k].wait()
        for m in range(MEMB):
            lat[k, :, m * cells : (m + 1) * cells] = (
                noise[k, m].astype(F32).reshape(flat, cells) * SIGMAS[0]
            )

    halo_copy.wait_recv()
    inside = jnp.where(top_half, tile > 0, tile < tiles - 1)
    from_neighbour = jnp.where(inside, halo_in[0:cin, :].astype(F32), 0.0)
    row_below = cv[:, half_rows, :].astype(F32)
    row_above = cv[:, half_rows - 1, :].astype(F32)
    edges = jnp.concatenate(
        [
            jnp.where(top_half, from_neighbour, row_above),
            jnp.where(top_half, row_below, from_neighbour),
        ],
        axis=1,
    ).astype(BF)
    lifted_edges = silu_of_half(jnp.dot(lift_bf, edges, preferred_element_type=F32))
    lifted[:channels, :cells] = lifted_edges[:, :cells]
    lifted[:channels, cells:] = lifted[octet * channels : (octet + 1) * channels, :cells]
    lifted[(octet + 1) * channels :, :cells] = lifted[channels : 2 * channels, cells:]
    lifted[(octet + 1) * channels :, cells:] = lifted_edges[:, cells:]
    column = lax.broadcasted_iota(jnp.int32, (channels, cells), 1)
    for r in range(octet):
        taps = jnp.dot(
            wconv[...],
            lifted[r * channels : (r + 3) * channels, :],
            preferred_element_type=F32,
        )
        for side in range(2):
            span = slice(side * cells, (side + 1) * cells)
            left = pltpu.roll(taps[:channels, span], 1, 1)
            right = pltpu.roll(taps[2 * channels :, span], cells - 1, 1)
            total = (
                taps[channels : 2 * channels, span]
                + jnp.where(column == 0, 0.0, left)
                + jnp.where(column == cells - 1, 0.0, right)
            )
            feat[r * channels : (r + 1) * channels, span] = silu_of_half(total)
    produced = jnp.dot(fout[...], feat[...], preferred_element_type=F32)
    condition = jnp.concatenate(
        [
            produced[c * octet : (c + 1) * octet, side * cells : (side + 1) * cells]
            for c in range(fields)
            for side in range(2)
        ],
        axis=0,
    ).astype(BF)

    lane_row = lax.broadcasted_iota(jnp.int32, (half_rows, cells), 1)
    listed = jnp.full((half_rows, cells), -1.0, F32)
    count = jnp.int32(MEMB)
    for j in range(REACH):
        listed = jnp.where(lane_row == j, dest_ref[0, j].astype(F32), listed)
        count = count + jnp.where(dest_ref[0, j] >= 0, 1, 0)
    cond[0, :flat, :] = condition
    cond[0, flat:, :] = listed.astype(BF)
    cond_copies = []
    for o in range(1, REACH):
        copy = pltpu.make_async_remote_copy(
            src_ref=cond.at[0],
            dst_ref=cond.at[o],
            send_sem=send_sem.at[o],
            recv_sem=recv_sem.at[o],
            device_id={"tile": ahead[o]},
            device_id_type=MESH,
        )
        copy.start()
        cond_copies.append(copy)

    def denoise_step(group, position):
        latent = lat[group]
        stacked = jnp.concatenate([(latent * pick(position, 0)).astype(BF), gx[group]], axis=0)
        piece_rows = 4 * channels
        for r in range(half_rows // 4):
            block = slice(r * piece_rows, (r + 1) * piece_rows)
            hid1[block, :] = silu_of_half(
                jnp.dot(ein[block, :], stacked, preferred_element_type=F32)
            )
        for r in range(half_rows // 2):
            block = slice(2 * r * channels, 2 * (r + 1) * channels)
            hid2[block, :] = silu_of_half(
                jnp.dot(emid[...], hid1[block, :], preferred_element_type=F32)
            )
        found = jnp.dot(eout[...], hid2[...], preferred_element_type=F32)
        lat[group] = latent * pick(position, 1) + found * pick(position, 2)

    def run_steps(group, low, high):
        def step(position, carry):
            denoise_step(group, position)
            return carry

        lax.fori_loop(low, high, step, 0)

    gx[0] = jnp.concatenate([condition] * MEMB, axis=1)
    run_steps(0, 0, NSTEP // 2)

    for copy in cond_copies:
        copy.wait_recv()
    me = tile.astype(F32)
    named = [
        jnp.max(jnp.where(cond[o, flat:, :].astype(F32) == me, 1.0, 0.0)) for o in range(REACH)
    ]
    chosen = []
    for o in range(REACH):
        rank = jnp.float32(0.0)
        for other in range(REACH):
            if other != o:
                rank = rank + jnp.where(behind[other] < behind[o], named[other], 0.0)
        chosen.append([jnp.where(rank == k, named[o], 0.0) for k in range(SLOTS)])
    for k in range(SLOTS):
        served = cond[0, :flat, :].astype(F32) * chosen[0][k]
        for o in range(1, REACH):
            served = served + cond[o, :flat, :].astype(F32) * chosen[o][k]
        gx[1, :, k * cells : (k + 1) * cells] = served.astype(BF)
    run_steps(1, 0, NSTEP)

    extra = lat[1] + gx[1].astype(F32)
    for o in range(REACH):
        sample = extra[:, :cells] * chosen[o][0]
        for k in range(1, SLOTS):
            sample = sample + extra[:, k * cells : (k + 1) * cells] * chosen[o][k]
        piece[o] = sample
    piece_copies = []
    for o in range(1, REACH):
        copy = pltpu.make_async_remote_copy(
            src_ref=piece.at[o],
            dst_ref=arrived.at[o],
            send_sem=send_sem.at[REACH + o],
            recv_sem=recv_sem.at[REACH + o],
            device_id={"tile": behind[o]},
            device_id_type=MESH,
        )
        copy.start()
        piece_copies.append(copy)

    run_steps(0, NSTEP // 2, NSTEP)

    base = lat[0] + gx[0].astype(F32)
    total = piece[0]
    square = total * total
    for m in range(MEMB):
        sample = base[:, m * cells : (m + 1) * cells]
        total = total + sample
        square = square + sample * sample
    for o, copy in enumerate(piece_copies, 1):
        copy.wait_recv()
        sample = arrived[o]
        total = total + sample
        square = square + sample * sample
    members = count.astype(F32)
    mean = total / members
    variance = square / members - mean * mean

    swap_out[...] = jnp.where(top_half, variance, mean)
    swap = pltpu.make_async_remote_copy(
        src_ref=swap_out,
        dst_ref=swap_in,
        send_sem=send_sem.at[REACH],
        recv_sem=recv_sem.at[REACH],
        device_id={"section": 1 - section},
        device_id_type=MESH,
    )
    swap.start()
    kept = jnp.where(top_half, mean, variance)
    out_ref[0, :, pl.ds(first, half_rows), :] = kept.reshape(fields, half_rows, cells)
    halo_copy.wait_send()
    for copy in cond_copies + piece_copies:
        copy.wait_send()
    swap.wait()
    second = pl.multiple_of((1 - section) * half_rows, half_rows)
    out_ref[0, :, pl.ds(second, half_rows), :] = swap_in[...].reshape(fields, half_rows, cells)


def body(tiles, *arrays):
    (coarse, lift, conv, outw, din, dmid, dout, base, slot, dest) = arrays
    cin, rows, cells = coarse.shape
    channels = lift.shape[0]
    fields = outw.shape[0]
    half = rows // 2
    flat = fields * half
    vmem = pl.BlockSpec(memory_space=pltpu.VMEM)
    anywhere = pl.BlockSpec(memory_space=pl.ANY)
    scratch = [
        pltpu.VMEM(coarse.shape, BF),
        pltpu.VMEM(conv.shape, BF),
        pltpu.VMEM((2, MEMB, fields, half, cells), BF),
        pltpu.VMEM((16, cells), BF),
        pltpu.VMEM((16, cells), BF),
        pltpu.VMEM(((half // 2 + 2) * channels, 2 * cells), BF),
        pltpu.VMEM((3 * channels, 3 * channels), BF),
        pltpu.VMEM((half // 2 * channels, 2 * cells), BF),
        pltpu.VMEM((fields * half // 2, half // 2 * channels), BF),
        pltpu.VMEM((half * channels, 2 * flat), BF),
        pltpu.VMEM((2 * channels, 2 * channels), BF),
        pltpu.VMEM((flat, half * channels), BF),
        pltpu.VMEM((half * channels, MEMB * cells), BF),
        pltpu.VMEM((half * channels, MEMB * cells), BF),
        pltpu.VMEM((2, flat, MEMB * cells), F32),
        pltpu.VMEM((REACH, flat + 16, cells), BF),
        pltpu.VMEM((2, flat, MEMB * cells), BF),
        pltpu.VMEM((REACH, flat, cells), F32),
        pltpu.VMEM((REACH, flat, cells), F32),
        pltpu.VMEM((flat, cells), F32),
        pltpu.VMEM((flat, cells), F32),
        pltpu.SemaphoreType.DMA((4,)),
        pltpu.SemaphoreType.DMA((2 * REACH,)),
        pltpu.SemaphoreType.DMA((2 * REACH,)),
    ]
    return pl.pallas_call(
        functools.partial(kernel, tiles),
        out_shape=jax.ShapeDtypeStruct((1, fields, rows, cells), F32),
        in_specs=[anywhere, vmem, anywhere, vmem, vmem, vmem, vmem, anywhere, anywhere]
        + [pl.BlockSpec(memory_space=pltpu.SMEM)],
        out_specs=vmem,
        scratch_shapes=scratch,
        compiler_params=pltpu.CompilerParams(
            collective_id=0, has_side_effects=True, vmem_limit_bytes=48 * 2**20
        ),
        name="ensemble",
    )(*arrays)


def solution(mesh):
    in_specs = (
        P(None, "tile", None),
        P(),
        P(),
        P(),
        P(),
        P(),
        P(),
        P(None, None, "tile", None),
        P(None, None, "tile", None),
        P("tile", None),
    )
    out_specs = P("section", None, "tile", None)
    return jax.shard_map(
        functools.partial(body, mesh.shape["tile"]),
        mesh=mesh,
        in_specs=in_specs,
        out_specs=out_specs,
        check_vma=False,
    )
```

```python
import functools
import math

import jax
import jax.numpy as jnp
from jax import lax
from jax.experimental import pallas as pl
from jax.experimental.pallas import tpu as pltpu
from jax.sharding import PartitionSpec as P

MESH = pl.DeviceIdType.MESH
BF = jnp.bfloat16
F32 = jnp.float32
MEMB = 4
SLOTS = 4
NSTEP = 6
REACH = 8
SIGMA_MAX = 4.0
SIGMA_MIN = 0.25
PLAN_POWER = 7.0


def sigma_table(step_count):
    upper_root = SIGMA_MAX ** (1.0 / PLAN_POWER)
    lower_root = SIGMA_MIN ** (1.0 / PLAN_POWER)
    values = []
    for position in range(step_count):
        fraction = position / (step_count - 1)
        values.append((upper_root + fraction * (lower_root - upper_root)) ** PLAN_POWER)
    values.append(0.0)
    return values


SIGMAS = sigma_table(NSTEP)


def step_factors():
    table = []
    for position in range(NSTEP):
        now, later = SIGMAS[position], SIGMAS[position + 1]
        scale = 1.0 / math.sqrt(now * now + 1.0)
        slope = (later - now) / now
        table.append((scale, 1.0 + slope * (1.0 - scale * scale), -slope * now * scale))
    return table


FACTORS = step_factors()


def pick(position, column):
    value = jnp.float32(FACTORS[NSTEP - 1][column])
    for step in range(NSTEP - 2, -1, -1):
        value = jnp.where(position == step, jnp.float32(FACTORS[step][column]), value)
    return value


def silu_of_half(half):
    return (half + half * jnp.tanh(half)).astype(BF)


def spread(rows, columns, by_row, group):
    i = lax.broadcasted_iota(jnp.int32, (rows, columns), 0)
    j = lax.broadcasted_iota(jnp.int32, (rows, columns), 1)
    same = (i // group == j) if by_row else (j // group == i)
    return same.astype(F32).astype(BF)


def kernel(
    tiles,
    coarse_ref,
    lift_ref,
    conv_ref,
    outw_ref,
    din_ref,
    dmid_ref,
    dout_ref,
    base_ref,
    slot_ref,
    dest_ref,
    out_ref,
    cv,
    wraw,
    lift_v,
    outw_v,
    din_v,
    dmid_v,
    dout_v,
    dest_s,
    noise,
    halo_out,
    halo_in,
    lifted,
    wconv,
    feat,
    fout,
    ein,
    emid,
    eout,
    hid1,
    hid2,
    lat,
    cond,
    gx,
    piece,
    arrived,
    swap_out,
    swap_in,
    local_sem,
    send_sem,
    recv_sem,
):
    section = lax.axis_index("section")
    tile = lax.axis_index("tile")
    half_rows = out_ref.shape[2] // 2
    cells = out_ref.shape[3]
    channels = din_ref.shape[1]
    fields = out_ref.shape[1]
    flat = fields * half_rows
    cin = lift_ref.shape[0]
    octet = half_rows // 2
    first = pl.multiple_of(section * half_rows, half_rows)

    copies = [
        pltpu.make_async_copy(coarse_ref, cv, local_sem.at[0]),
        pltpu.make_async_copy(conv_ref, wraw, local_sem.at[1]),
        pltpu.make_async_copy(
            base_ref.at[:, :, pl.ds(first, half_rows), :], noise.at[0], local_sem.at[2]
        ),
        pltpu.make_async_copy(
            slot_ref.at[:, :, pl.ds(first, half_rows), :], noise.at[1], local_sem.at[3]
        ),
        pltpu.make_async_copy(lift_ref, lift_v, local_sem.at[4]),
        pltpu.make_async_copy(outw_ref, outw_v, local_sem.at[5]),
        pltpu.make_async_copy(din_ref, din_v, local_sem.at[6]),
        pltpu.make_async_copy(dmid_ref, dmid_v, local_sem.at[7]),
        pltpu.make_async_copy(dout_ref, dout_v, local_sem.at[8]),
        pltpu.make_async_copy(dest_ref, dest_s, local_sem.at[9]),
    ]
    for copy in copies:
        copy.start()

    ahead = [lax.rem(tile + o, tiles) for o in range(REACH)]
    behind = [lax.rem(tile + tiles - o, tiles) for o in range(REACH)]

    barrier = pltpu.get_barrier_semaphore()
    for o in range(1, REACH):
        for other in (ahead[o], behind[o]):
            pl.semaphore_signal(barrier, inc=1, device_id={"tile": other}, device_id_type=MESH)
    pl.semaphore_signal(
        barrier, inc=1, device_id={"section": 1 - section}, device_id_type=MESH
    )

    copies[0].wait()
    top_half = section == 0
    last_row = cv[:, 2 * half_rows - 1, :].astype(F32)
    first_row = cv[:, 0, :].astype(F32)
    halo_out[...] = jnp.zeros(halo_out.shape, BF)
    halo_out[0:cin, :] = jnp.where(top_half, last_row, first_row).astype(BF)

    pl.semaphore_wait(barrier, 2 * (REACH - 1) + 1)
    halo_target = lax.rem(jnp.where(top_half, tile + 1, tile + tiles - 1), tiles)
    halo_copy = pltpu.make_async_remote_copy(
        src_ref=halo_out,
        dst_ref=halo_in,
        send_sem=send_sem.at[0],
        recv_sem=recv_sem.at[0],
        device_id={"tile": halo_target},
        device_id_type=MESH,
    )
    halo_copy.start()

    for copy in copies[4:]:
        copy.wait()
    lift_half = lift_v[...].astype(F32) * 0.5
    lift_bf = lift_half.T.astype(BF)
    wide = jnp.dot(lift_bf, spread(cin, cin * octet, False, octet), preferred_element_type=F32)
    lane = lax.broadcasted_iota(jnp.int32, wide.shape, 1) % octet
    own = cv[:, pl.ds(first, half_rows), :].astype(F32)
    own = jnp.concatenate(
        [
            own[:, :octet, :].reshape(cin * octet, cells),
            own[:, octet:, :].reshape(cin * octet, cells),
        ],
        axis=1,
    ).astype(BF)
    for r in range(octet):
        weight = jnp.where(lane == r, wide, 0.0).astype(BF)
        lifted[(r + 1) * channels : (r + 2) * channels, :] = silu_of_half(
            jnp.dot(weight, own, preferred_element_type=F32)
        )
    copies[1].wait()
    for a in range(3):
        for b in range(3):
            wconv[b * channels : (b + 1) * channels, a * channels : (a + 1) * channels] = (
                (wraw[a, b].astype(F32) * 0.5).T.astype(BF)
            )
    wide_in = (
        jnp.dot(
            din_v[...].astype(F32).T.astype(BF), spread(2 * fields, 2 * flat, False, half_rows), preferred_element_type=F32
        )
        * 0.5
    )
    lane_in = lax.broadcasted_iota(jnp.int32, wide_in.shape, 1) % half_rows
    wide_out = jnp.dot(
        spread(flat, fields, True, half_rows), dout_v[...], preferred_element_type=F32
    )
    row_out = lax.broadcasted_iota(jnp.int32, wide_out.shape, 0) % half_rows
    for r in range(half_rows):
        block = slice(r * channels, (r + 1) * channels)
        ein[block, :] = jnp.where(lane_in == r, wide_in, 0.0).astype(BF)
        eout[:, block] = jnp.where(row_out == r, wide_out, 0.0).astype(BF)
    mid = (dmid_v[...].astype(F32) * 0.5).astype(BF)
    emid[...] = jnp.zeros(emid.shape, BF)
    emid[:channels, :channels] = mid
    emid[channels:, channels:] = mid
    wide_reg = jnp.dot(
        spread(fields * octet, fields, True, octet), outw_v[...], preferred_element_type=F32
    )
    row_reg = lax.broadcasted_iota(jnp.int32, wide_reg.shape, 0) % octet
    for r in range(octet):
        fout[:, r * channels : (r + 1) * channels] = jnp.where(row_reg == r, wide_reg, 0.0).astype(
            BF
        )
    for k in range(2):
        copies[2 + k].wait()
        for m in range(MEMB):
            lat[k, :, m * cells : (m + 1) * cells] = (
                noise[k, m].astype(F32).reshape(flat, cells) * SIGMAS[0]
            )

    halo_copy.wait_recv()
    inside = jnp.where(top_half, tile > 0, tile < tiles - 1)
    from_neighbour = jnp.where(inside, halo_in[0:cin, :].astype(F32), 0.0)
    row_below = cv[:, half_rows, :].astype(F32)
    row_above = cv[:, half_rows - 1, :].astype(F32)
    edges = jnp.concatenate(
        [
            jnp.where(top_half, from_neighbour, row_above),
            jnp.where(top_half, row_below, from_neighbour),
        ],
        axis=1,
    ).astype(BF)
    lifted_edges = silu_of_half(jnp.dot(lift_bf, edges, preferred_element_type=F32))
    lifted[:channels, :cells] = lifted_edges[:, :cells]
    lifted[:channels, cells:] = lifted[octet * channels : (octet + 1) * channels, :cells]
    lifted[(octet + 1) * channels :, :cells] = lifted[channels : 2 * channels, cells:]
    lifted[(octet + 1) * channels :, cells:] = lifted_edges[:, cells:]
    column = lax.broadcasted_iota(jnp.int32, (channels, cells), 1)
    for r in range(octet):
        taps = jnp.dot(
            wconv[...],
            lifted[r * channels : (r + 3) * channels, :],
            preferred_element_type=F32,
        )
        for side in range(2):
            span = slice(side * cells, (side + 1) * cells)
            left = pltpu.roll(taps[:channels, span], 1, 1)
            right = pltpu.roll(taps[2 * channels :, span], cells - 1, 1)
            total = (
                taps[channels : 2 * channels, span]
                + jnp.where(column == 0, 0.0, left)
                + jnp.where(column == cells - 1, 0.0, right)
            )
            feat[r * channels : (r + 1) * channels, span] = silu_of_half(total)
    produced = jnp.dot(fout[...], feat[...], preferred_element_type=F32)
    condition = jnp.concatenate(
        [
            produced[c * octet : (c + 1) * octet, side * cells : (side + 1) * cells]
            for c in range(fields)
            for side in range(2)
        ],
        axis=0,
    ).astype(BF)

    lane_row = lax.broadcasted_iota(jnp.int32, (half_rows, cells), 1)
    listed = jnp.full((half_rows, cells), -1.0, F32)
    count = jnp.int32(MEMB)
    for j in range(REACH):
        listed = jnp.where(lane_row == j, dest_s[0, j].astype(F32), listed)
        count = count + jnp.where(dest_s[0, j] >= 0, 1, 0)
    cond[0, :flat, :] = condition
    cond[0, flat:, :] = listed.astype(BF)
    cond_copies = []
    for o in range(1, REACH):
        copy = pltpu.make_async_remote_copy(
            src_ref=cond.at[0],
            dst_ref=cond.at[o],
            send_sem=send_sem.at[o],
            recv_sem=recv_sem.at[o],
            device_id={"tile": ahead[o]},
            device_id_type=MESH,
        )
        copy.start()
        cond_copies.append(copy)

    def denoise_step(group, position):
        latent = lat[group]
        stacked = jnp.concatenate([(latent * pick(position, 0)).astype(BF), gx[group]], axis=0)
        piece_rows = 4 * channels
        for r in range(half_rows // 4):
            block = slice(r * piece_rows, (r + 1) * piece_rows)
            hid1[block, :] = silu_of_half(
                jnp.dot(ein[block, :], stacked, preferred_element_type=F32)
            )
        for r in range(half_rows // 2):
            block = slice(2 * r * channels, 2 * (r + 1) * channels)
            hid2[block, :] = silu_of_half(
                jnp.dot(emid[...], hid1[block, :], preferred_element_type=F32)
            )
        found = jnp.dot(eout[...], hid2[...], preferred_element_type=F32)
        lat[group] = latent * pick(position, 1) + found * pick(position, 2)

    def run_steps(group, low, high):
        def step(position, carry):
            denoise_step(group, position)
            return carry

        lax.fori_loop(low, high, step, 0)

    gx[0] = jnp.concatenate([condition] * MEMB, axis=1)
    run_steps(0, 0, NSTEP // 2)

    for copy in cond_copies:
        copy.wait_recv()
    me = tile.astype(F32)
    named = [
        jnp.max(jnp.where(cond[o, flat:, :].astype(F32) == me, 1.0, 0.0)) for o in range(REACH)
    ]
    chosen = []
    for o in range(REACH):
        rank = jnp.float32(0.0)
        for other in range(REACH):
            if other != o:
                rank = rank + jnp.where(behind[other] < behind[o], named[other], 0.0)
        chosen.append([jnp.where(rank == k, named[o], 0.0) for k in range(SLOTS)])
    for k in range(SLOTS):
        served = cond[0, :flat, :].astype(F32) * chosen[0][k]
        for o in range(1, REACH):
            served = served + cond[o, :flat, :].astype(F32) * chosen[o][k]
        gx[1, :, k * cells : (k + 1) * cells] = served.astype(BF)
    run_steps(1, 0, NSTEP)

    extra = lat[1] + gx[1].astype(F32)
    for o in range(REACH):
        sample = extra[:, :cells] * chosen[o][0]
        for k in range(1, SLOTS):
            sample = sample + extra[:, k * cells : (k + 1) * cells] * chosen[o][k]
        piece[o] = sample
    piece_copies = []
    for o in range(1, REACH):
        copy = pltpu.make_async_remote_copy(
            src_ref=piece.at[o],
            dst_ref=arrived.at[o],
            send_sem=send_sem.at[REACH + o],
            recv_sem=recv_sem.at[REACH + o],
            device_id={"tile": behind[o]},
            device_id_type=MESH,
        )
        copy.start()
        piece_copies.append(copy)

    run_steps(0, NSTEP // 2, NSTEP)

    base = lat[0] + gx[0].astype(F32)
    total = piece[0]
    square = total * total
    for m in range(MEMB):
        sample = base[:, m * cells : (m + 1) * cells]
        total = total + sample
        square = square + sample * sample
    for o, copy in enumerate(piece_copies, 1):
        copy.wait_recv()
        sample = arrived[o]
        total = total + sample
        square = square + sample * sample
    members = count.astype(F32)
    mean = total / members
    variance = square / members - mean * mean

    swap_out[...] = jnp.where(top_half, variance, mean)
    swap = pltpu.make_async_remote_copy(
        src_ref=swap_out,
        dst_ref=swap_in,
        send_sem=send_sem.at[REACH],
        recv_sem=recv_sem.at[REACH],
        device_id={"section": 1 - section},
        device_id_type=MESH,
    )
    swap.start()
    kept = jnp.where(top_half, mean, variance)
    out_ref[0, :, pl.ds(first, half_rows), :] = kept.reshape(fields, half_rows, cells)
    halo_copy.wait_send()
    for copy in cond_copies + piece_copies:
        copy.wait_send()
    swap.wait()
    second = pl.multiple_of((1 - section) * half_rows, half_rows)
    out_ref[0, :, pl.ds(second, half_rows), :] = swap_in[...].reshape(fields, half_rows, cells)


def body(tiles, *arrays):
    (coarse, lift, conv, outw, din, dmid, dout, base, slot, dest) = arrays
    cin, rows, cells = coarse.shape
    channels = lift.shape[0]
    lift = lift.T
    din = din.T
    fields = outw.shape[0]
    half = rows // 2
    flat = fields * half
    vmem = pl.BlockSpec(memory_space=pltpu.VMEM)
    in_hbm = pl.BlockSpec(memory_space=pltpu.HBM)
    scratch = [
        pltpu.VMEM(coarse.shape, BF),
        pltpu.VMEM(conv.shape, BF),
        pltpu.VMEM(lift.shape, BF),
        pltpu.VMEM(outw.shape, BF),
        pltpu.VMEM(din.shape, BF),
        pltpu.VMEM(dmid.shape, BF),
        pltpu.VMEM(dout.shape, BF),
        pltpu.SMEM(dest.shape, jnp.int32),
        pltpu.VMEM((2, MEMB, fields, half, cells), BF),
        pltpu.VMEM((16, cells), BF),
        pltpu.VMEM((16, cells), BF),
        pltpu.VMEM(((half // 2 + 2) * channels, 2 * cells), BF),
        pltpu.VMEM((3 * channels, 3 * channels), BF),
        pltpu.VMEM((half // 2 * channels, 2 * cells), BF),
        pltpu.VMEM((fields * half // 2, half // 2 * channels), BF),
        pltpu.VMEM((half * channels, 2 * flat), BF),
        pltpu.VMEM((2 * channels, 2 * channels), BF),
        pltpu.VMEM((flat, half * channels), BF),
        pltpu.VMEM((half * channels, MEMB * cells), BF),
        pltpu.VMEM((half * channels, MEMB * cells), BF),
        pltpu.VMEM((2, flat, MEMB * cells), F32),
        pltpu.VMEM((REACH, flat + 16, cells), BF),
        pltpu.VMEM((2, flat, MEMB * cells), BF),
        pltpu.VMEM((REACH, flat, cells), F32),
        pltpu.VMEM((REACH, flat, cells), F32),
        pltpu.VMEM((flat, cells), F32),
        pltpu.VMEM((flat, cells), F32),
        pltpu.SemaphoreType.DMA((10,)),
        pltpu.SemaphoreType.DMA((2 * REACH,)),
        pltpu.SemaphoreType.DMA((2 * REACH,)),
    ]
    return pl.pallas_call(
        functools.partial(kernel, tiles),
        out_shape=jax.ShapeDtypeStruct((1, fields, rows, cells), F32),
        in_specs=[in_hbm] * 10,
        out_specs=vmem,
        scratch_shapes=scratch,
        compiler_params=pltpu.CompilerParams(
            collective_id=0, has_side_effects=True, vmem_limit_bytes=60 * 2**20
        ),
        name="ensemble",
    )(coarse, lift, conv, outw, din, dmid, dout, base, slot, dest)


def solution(mesh):
    in_specs = (
        P(None, "tile", None),
        P(),
        P(),
        P(),
        P(),
        P(),
        P(),
        P(None, None, "tile", None),
        P(None, None, "tile", None),
        P("tile", None),
    )
    out_specs = P("section", None, "tile", None)
    return jax.shard_map(
        functools.partial(body, mesh.shape["tile"]),
        mesh=mesh,
        in_specs=in_specs,
        out_specs=out_specs,
        check_vma=False,
    )
```

```python
import functools
import math

import jax
import jax.numpy as jnp
from jax import lax
from jax.experimental import pallas as pl
from jax.experimental.pallas import tpu as pltpu
from jax.sharding import PartitionSpec as P

MESH = pl.DeviceIdType.MESH
BF = jnp.bfloat16
F32 = jnp.float32
MEMB = 4
SLOTS = 4
NSTEP = 6
REACH = 8
SIGMA_MAX = 4.0
SIGMA_MIN = 0.25
PLAN_POWER = 7.0


def sigma_table(step_count):
    upper_root = SIGMA_MAX ** (1.0 / PLAN_POWER)
    lower_root = SIGMA_MIN ** (1.0 / PLAN_POWER)
    values = []
    for position in range(step_count):
        fraction = position / (step_count - 1)
        values.append((upper_root + fraction * (lower_root - upper_root)) ** PLAN_POWER)
    values.append(0.0)
    return values


SIGMAS = sigma_table(NSTEP)


def step_factors():
    table = []
    for position in range(NSTEP):
        now, later = SIGMAS[position], SIGMAS[position + 1]
        scale = 1.0 / math.sqrt(now * now + 1.0)
        slope = (later - now) / now
        table.append((scale, 1.0 + slope * (1.0 - scale * scale), -slope * now * scale))
    return table


FACTORS = step_factors()


def pick(position, column):
    value = jnp.float32(FACTORS[NSTEP - 1][column])
    for step in range(NSTEP - 2, -1, -1):
        value = jnp.where(position == step, jnp.float32(FACTORS[step][column]), value)
    return value


def silu_of_half(half):
    return (half + half * jnp.tanh(half)).astype(BF)


def spread(rows, columns, by_row, group):
    i = lax.broadcasted_iota(jnp.int32, (rows, columns), 0)
    j = lax.broadcasted_iota(jnp.int32, (rows, columns), 1)
    same = (i // group == j) if by_row else (j // group == i)
    return same.astype(F32).astype(BF)


def kernel(
    tiles,
    coarse_ref,
    lift_ref,
    conv_ref,
    outw_ref,
    din_ref,
    dmid_ref,
    dout_ref,
    base_ref,
    slot_ref,
    dest_ref,
    out_ref,
    cv,
    wraw,
    lift_v,
    outw_v,
    din_v,
    dmid_v,
    dout_v,
    dest_s,
    noise,
    halo_out,
    halo_in,
    lifted,
    wconv,
    feat,
    fout,
    ein,
    emid,
    eout,
    hid1,
    hid2,
    lat,
    cond,
    listing,
    gx,
    piece,
    arrived,
    swap_out,
    swap_in,
    local_sem,
    send_sem,
    recv_sem,
):
    section = lax.axis_index("section")
    tile = lax.axis_index("tile")
    half_rows = out_ref.shape[2] // 2
    cells = out_ref.shape[3]
    channels = din_ref.shape[1]
    fields = out_ref.shape[1]
    flat = fields * half_rows
    cin = lift_ref.shape[0]
    octet = half_rows // 2
    first = pl.multiple_of(section * half_rows, half_rows)

    copies = [
        pltpu.make_async_copy(coarse_ref, cv, local_sem.at[0]),
        pltpu.make_async_copy(conv_ref, wraw, local_sem.at[1]),
        pltpu.make_async_copy(
            base_ref.at[:, :, pl.ds(first, half_rows), :], noise.at[0], local_sem.at[2]
        ),
        pltpu.make_async_copy(
            slot_ref.at[:, :, pl.ds(first, half_rows), :], noise.at[1], local_sem.at[3]
        ),
        pltpu.make_async_copy(lift_ref, lift_v, local_sem.at[4]),
        pltpu.make_async_copy(outw_ref, outw_v, local_sem.at[5]),
        pltpu.make_async_copy(din_ref, din_v, local_sem.at[6]),
        pltpu.make_async_copy(dmid_ref, dmid_v, local_sem.at[7]),
        pltpu.make_async_copy(dout_ref, dout_v, local_sem.at[8]),
        pltpu.make_async_copy(dest_ref, dest_s, local_sem.at[9]),
    ]
    for copy in copies:
        copy.start()

    ahead = [lax.rem(tile + o, tiles) for o in range(REACH)]
    behind = [lax.rem(tile + tiles - o, tiles) for o in range(REACH)]

    barrier = pltpu.get_barrier_semaphore()
    for o in range(REACH - 1, 0, -1):
        for other in (ahead[o], behind[o]):
            pl.semaphore_signal(barrier, inc=1, device_id={"tile": other}, device_id_type=MESH)
    pl.semaphore_signal(
        barrier, inc=1, device_id={"section": 1 - section}, device_id_type=MESH
    )

    copies[0].wait()
    top_half = section == 0
    last_row = cv[:, 2 * half_rows - 1, :].astype(F32)
    first_row = cv[:, 0, :].astype(F32)
    halo_out[...] = jnp.zeros(halo_out.shape, BF)
    halo_out[0:cin, :] = jnp.where(top_half, last_row, first_row).astype(BF)

    for copy in copies[4:]:
        copy.wait()
    lift_half = lift_v[...].astype(F32) * 0.5
    lift_bf = lift_half.T.astype(BF)
    wide = jnp.dot(lift_bf, spread(cin, cin * octet, False, octet), preferred_element_type=F32)
    lane = lax.broadcasted_iota(jnp.int32, wide.shape, 1) % octet
    own = cv[:, pl.ds(first, half_rows), :].astype(F32)
    own = jnp.concatenate(
        [
            own[:, :octet, :].reshape(cin * octet, cells),
            own[:, octet:, :].reshape(cin * octet, cells),
        ],
        axis=1,
    ).astype(BF)
    for r in range(octet):
        weight = jnp.where(lane == r, wide, 0.0).astype(BF)
        lifted[(r + 1) * channels : (r + 2) * channels, :] = silu_of_half(
            jnp.dot(weight, own, preferred_element_type=F32)
        )
    copies[1].wait()
    for a in range(3):
        for b in range(3):
            wconv[b * channels : (b + 1) * channels, a * channels : (a + 1) * channels] = (
                (wraw[a, b].astype(F32) * 0.5).T.astype(BF)
            )
    wide_reg = jnp.dot(
        spread(fields * octet, fields, True, octet), outw_v[...], preferred_element_type=F32
    )
    row_reg = lax.broadcasted_iota(jnp.int32, wide_reg.shape, 0) % octet
    for r in range(octet):
        fout[:, r * channels : (r + 1) * channels] = jnp.where(row_reg == r, wide_reg, 0.0).astype(
            BF
        )
    pl.semaphore_wait(barrier, 2 * (REACH - 1) + 1)
    halo_target = lax.rem(jnp.where(top_half, tile + 1, tile + tiles - 1), tiles)
    halo_copy = pltpu.make_async_remote_copy(
        src_ref=halo_out,
        dst_ref=halo_in,
        send_sem=send_sem.at[0],
        recv_sem=recv_sem.at[0],
        device_id={"tile": halo_target},
        device_id_type=MESH,
    )
    halo_copy.start()

    lane_row = lax.broadcasted_iota(jnp.int32, (8, cells), 1)
    listed = jnp.full((8, cells), -1.0, F32)
    count = jnp.int32(MEMB)
    for j in range(REACH):
        listed = jnp.where(lane_row == j, dest_s[0, j].astype(F32), listed)
        count = count + jnp.where(dest_s[0, j] >= 0, 1, 0)
    listing[0] = listed
    list_copies = []
    for o in range(REACH - 1, 0, -1):
        copy = pltpu.make_async_remote_copy(
            src_ref=listing.at[0],
            dst_ref=listing.at[o],
            send_sem=send_sem.at[2 * REACH + o],
            recv_sem=recv_sem.at[2 * REACH + o],
            device_id={"tile": ahead[o]},
            device_id_type=MESH,
        )
        copy.start()
        list_copies.append(copy)

    column = lax.broadcasted_iota(jnp.int32, (channels, cells), 1)

    def convolve(r):
        taps = jnp.dot(
            wconv[...],
            lifted[r * channels : (r + 3) * channels, :],
            preferred_element_type=F32,
        )
        for side in range(2):
            span = slice(side * cells, (side + 1) * cells)
            left = pltpu.roll(taps[:channels, span], 1, 1)
            right = pltpu.roll(taps[2 * channels :, span], cells - 1, 1)
            total = (
                taps[channels : 2 * channels, span]
                + jnp.where(column == 0, 0.0, left)
                + jnp.where(column == cells - 1, 0.0, right)
            )
            feat[r * channels : (r + 1) * channels, span] = silu_of_half(total)

    for r in range(1, octet - 1):
        convolve(r)

    halo_copy.wait_recv()
    inside = jnp.where(top_half, tile > 0, tile < tiles - 1)
    from_neighbour = jnp.where(inside, halo_in[0:cin, :].astype(F32), 0.0)
    row_below = cv[:, half_rows, :].astype(F32)
    row_above = cv[:, half_rows - 1, :].astype(F32)
    edges = jnp.concatenate(
        [
            jnp.where(top_half, from_neighbour, row_above),
            jnp.where(top_half, row_below, from_neighbour),
        ],
        axis=1,
    ).astype(BF)
    lifted_edges = silu_of_half(jnp.dot(lift_bf, edges, preferred_element_type=F32))
    lifted[:channels, :cells] = lifted_edges[:, :cells]
    lifted[:channels, cells:] = lifted[octet * channels : (octet + 1) * channels, :cells]
    lifted[(octet + 1) * channels :, :cells] = lifted[channels : 2 * channels, cells:]
    lifted[(octet + 1) * channels :, cells:] = lifted_edges[:, cells:]
    convolve(0)
    convolve(octet - 1)
    produced = jnp.dot(fout[...], feat[...], preferred_element_type=F32)
    condition = jnp.concatenate(
        [
            produced[c * octet : (c + 1) * octet, side * cells : (side + 1) * cells]
            for c in range(fields)
            for side in range(2)
        ],
        axis=0,
    ).astype(BF)

    cond[0] = condition
    cond_copies = []
    for o in range(REACH - 1, 0, -1):
        copy = pltpu.make_async_remote_copy(
            src_ref=cond.at[0],
            dst_ref=cond.at[o],
            send_sem=send_sem.at[o],
            recv_sem=recv_sem.at[o],
            device_id={"tile": ahead[o]},
            device_id_type=MESH,
        )
        copy.start()
        cond_copies.append(copy)

    wide_in = (
        jnp.dot(
            din_v[...].astype(F32).T.astype(BF),
            spread(2 * fields, 2 * flat, False, half_rows),
            preferred_element_type=F32,
        )
        * 0.5
    )
    lane_in = lax.broadcasted_iota(jnp.int32, wide_in.shape, 1) % half_rows
    wide_out = jnp.dot(
        spread(flat, fields, True, half_rows), dout_v[...], preferred_element_type=F32
    )
    row_out = lax.broadcasted_iota(jnp.int32, wide_out.shape, 0) % half_rows
    for r in range(half_rows):
        block = slice(r * channels, (r + 1) * channels)
        ein[block, :] = jnp.where(lane_in == r, wide_in, 0.0).astype(BF)
        eout[:, block] = jnp.where(row_out == r, wide_out, 0.0).astype(BF)
    mid = (dmid_v[...].astype(F32) * 0.5).astype(BF)
    emid[...] = jnp.zeros(emid.shape, BF)
    emid[:channels, :channels] = mid
    emid[channels:, channels:] = mid
    for k in range(2):
        copies[2 + k].wait()
        for m in range(MEMB):
            lat[k, :, m * cells : (m + 1) * cells] = (
                noise[k, m].astype(F32).reshape(flat, cells) * SIGMAS[0]
            )

    def denoise_step(group, position):
        latent = lat[group]
        stacked = jnp.concatenate([(latent * pick(position, 0)).astype(BF), gx[group]], axis=0)
        piece_rows = 4 * channels
        for r in range(half_rows // 4):
            block = slice(r * piece_rows, (r + 1) * piece_rows)
            hid1[block, :] = silu_of_half(
                jnp.dot(ein[block, :], stacked, preferred_element_type=F32)
            )
        for r in range(half_rows // 2):
            block = slice(2 * r * channels, 2 * (r + 1) * channels)
            hid2[block, :] = silu_of_half(
                jnp.dot(emid[...], hid1[block, :], preferred_element_type=F32)
            )
        found = jnp.dot(eout[...], hid2[...], preferred_element_type=F32)
        lat[group] = latent * pick(position, 1) + found * pick(position, 2)

    def run_steps(group, low, high):
        def step(position, carry):
            denoise_step(group, position)
            return carry

        lax.fori_loop(low, high, step, 0)

    gx[0] = jnp.concatenate([condition] * MEMB, axis=1)
    run_steps(0, 0, 4)

    for copy in list_copies + cond_copies:
        copy.wait_recv()
    me = tile.astype(F32)
    named = [
        jnp.max(jnp.where(listing[o] == me, 1.0, 0.0)) for o in range(REACH)
    ]
    chosen = []
    for o in range(REACH):
        rank = jnp.float32(0.0)
        for other in range(REACH):
            if other != o:
                rank = rank + jnp.where(behind[other] < behind[o], named[other], 0.0)
        chosen.append([jnp.where(rank == k, named[o], 0.0) for k in range(SLOTS)])
    for k in range(SLOTS):
        served = cond[0].astype(F32) * chosen[0][k]
        for o in range(1, REACH):
            served = served + cond[o].astype(F32) * chosen[o][k]
        gx[1, :, k * cells : (k + 1) * cells] = served.astype(BF)
    run_steps(1, 0, NSTEP)

    extra = lat[1] + gx[1].astype(F32)
    own_sample = None
    piece_copies = []
    for o in range(REACH - 1, -1, -1):
        sample = extra[:, :cells] * chosen[o][0]
        for k in range(1, SLOTS):
            sample = sample + extra[:, k * cells : (k + 1) * cells] * chosen[o][k]
        if o == 0:
            own_sample = sample
            continue
        piece[o] = sample.astype(BF)
        copy = pltpu.make_async_remote_copy(
            src_ref=piece.at[o],
            dst_ref=arrived.at[o],
            send_sem=send_sem.at[REACH + o],
            recv_sem=recv_sem.at[REACH + o],
            device_id={"tile": behind[o]},
            device_id_type=MESH,
        )
        copy.start()
        piece_copies.append(copy)

    run_steps(0, 4, NSTEP)

    base = lat[0] + gx[0].astype(F32)
    total = own_sample
    square = total * total
    for m in range(MEMB):
        sample = base[:, m * cells : (m + 1) * cells]
        total = total + sample
        square = square + sample * sample
    for o in range(1, REACH):
        piece_copies[REACH - 1 - o].wait_recv()
        sample = arrived[o].astype(F32)
        total = total + sample
        square = square + sample * sample
    members = count.astype(F32)
    mean = total / members
    variance = square / members - mean * mean

    swap_out[...] = jnp.where(top_half, variance, mean)
    swap = pltpu.make_async_remote_copy(
        src_ref=swap_out,
        dst_ref=swap_in,
        send_sem=send_sem.at[REACH],
        recv_sem=recv_sem.at[REACH],
        device_id={"section": 1 - section},
        device_id_type=MESH,
    )
    swap.start()
    kept = jnp.where(top_half, mean, variance)
    out_ref[0, :, pl.ds(first, half_rows), :] = kept.reshape(fields, half_rows, cells)
    halo_copy.wait_send()
    for copy in list_copies + cond_copies + piece_copies:
        copy.wait_send()
    swap.wait()
    second = pl.multiple_of((1 - section) * half_rows, half_rows)
    out_ref[0, :, pl.ds(second, half_rows), :] = swap_in[...].reshape(fields, half_rows, cells)


def body(tiles, *arrays):
    (coarse, lift, conv, outw, din, dmid, dout, base, slot, dest) = arrays
    cin, rows, cells = coarse.shape
    channels = lift.shape[0]
    lift = lift.T
    din = din.T
    fields = outw.shape[0]
    half = rows // 2
    flat = fields * half
    vmem = pl.BlockSpec(memory_space=pltpu.VMEM)
    in_hbm = pl.BlockSpec(memory_space=pltpu.HBM)
    scratch = [
        pltpu.VMEM(coarse.shape, BF),
        pltpu.VMEM(conv.shape, BF),
        pltpu.VMEM(lift.shape, BF),
        pltpu.VMEM(outw.shape, BF),
        pltpu.VMEM(din.shape, BF),
        pltpu.VMEM(dmid.shape, BF),
        pltpu.VMEM(dout.shape, BF),
        pltpu.SMEM(dest.shape, jnp.int32),
        pltpu.VMEM((2, MEMB, fields, half, cells), BF),
        pltpu.VMEM((16, cells), BF),
        pltpu.VMEM((16, cells), BF),
        pltpu.VMEM(((half // 2 + 2) * channels, 2 * cells), BF),
        pltpu.VMEM((3 * channels, 3 * channels), BF),
        pltpu.VMEM((half // 2 * channels, 2 * cells), BF),
        pltpu.VMEM((fields * half // 2, half // 2 * channels), BF),
        pltpu.VMEM((half * channels, 2 * flat), BF),
        pltpu.VMEM((2 * channels, 2 * channels), BF),
        pltpu.VMEM((flat, half * channels), BF),
        pltpu.VMEM((half * channels, MEMB * cells), BF),
        pltpu.VMEM((half * channels, MEMB * cells), BF),
        pltpu.VMEM((2, flat, MEMB * cells), F32),
        pltpu.VMEM((REACH, flat, cells), BF),
        pltpu.VMEM((REACH, 8, cells), F32),
        pltpu.VMEM((2, flat, MEMB * cells), BF),
        pltpu.VMEM((REACH, flat, cells), BF),
        pltpu.VMEM((REACH, flat, cells), BF),
        pltpu.VMEM((flat, cells), F32),
        pltpu.VMEM((flat, cells), F32),
        pltpu.SemaphoreType.DMA((10,)),
        pltpu.SemaphoreType.DMA((3 * REACH,)),
        pltpu.SemaphoreType.DMA((3 * REACH,)),
    ]
    return pl.pallas_call(
        functools.partial(kernel, tiles),
        out_shape=jax.ShapeDtypeStruct((1, fields, rows, cells), F32),
        in_specs=[in_hbm] * 10,
        out_specs=vmem,
        scratch_shapes=scratch,
        compiler_params=pltpu.CompilerParams(
            collective_id=0, has_side_effects=True, vmem_limit_bytes=48 * 2**20
        ),
        name="ensemble",
    )(
        *[
            pltpu.with_memory_space_constraint(array, pltpu.HBM)
            for array in (coarse, lift, conv, outw, din, dmid, dout, base, slot, dest)
        ]
    )


def solution(mesh):
    in_specs = (
        P(None, "tile", None),
        P(),
        P(),
        P(),
        P(),
        P(),
        P(),
        P(None, None, "tile", None),
        P(None, None, "tile", None),
        P("tile", None),
    )
    out_specs = P("section", None, "tile", None)
    return jax.shard_map(
        functools.partial(body, mesh.shape["tile"]),
        mesh=mesh,
        in_specs=in_specs,
        out_specs=out_specs,
        check_vma=False,
    )
```

```python
import functools
import math

import jax
import jax.numpy as jnp
from jax import lax
from jax.experimental import pallas as pl
from jax.experimental.pallas import tpu as pltpu
from jax.sharding import PartitionSpec as P

MESH = pl.DeviceIdType.MESH
BF = jnp.bfloat16
F32 = jnp.float32
MEMB = 4
SLOTS = 4
NSTEP = 6
REACH = 8
SIGMA_MAX = 4.0
SIGMA_MIN = 0.25
PLAN_POWER = 7.0


def sigma_table(step_count):
    upper_root = SIGMA_MAX ** (1.0 / PLAN_POWER)
    lower_root = SIGMA_MIN ** (1.0 / PLAN_POWER)
    values = []
    for position in range(step_count):
        fraction = position / (step_count - 1)
        values.append((upper_root + fraction * (lower_root - upper_root)) ** PLAN_POWER)
    values.append(0.0)
    return values


SIGMAS = sigma_table(NSTEP)


def step_factors():
    table = []
    for position in range(NSTEP):
        now, later = SIGMAS[position], SIGMAS[position + 1]
        scale = 1.0 / math.sqrt(now * now + 1.0)
        slope = (later - now) / now
        table.append((scale, 1.0 + slope * (1.0 - scale * scale), -slope * now * scale))
    return table


FACTORS = step_factors()


def pick(position, column):
    value = jnp.float32(FACTORS[NSTEP - 1][column])
    for step in range(NSTEP - 2, -1, -1):
        value = jnp.where(position == step, jnp.float32(FACTORS[step][column]), value)
    return value


def silu_of_half(half):
    return (half + half * jnp.tanh(half)).astype(BF)


def spread(rows, columns, by_row, group):
    i = lax.broadcasted_iota(jnp.int32, (rows, columns), 0)
    j = lax.broadcasted_iota(jnp.int32, (rows, columns), 1)
    same = (i // group == j) if by_row else (j // group == i)
    return same.astype(F32).astype(BF)


def kernel(
    tiles,
    coarse_ref,
    lift_ref,
    conv_ref,
    outw_ref,
    din_ref,
    dmid_ref,
    dout_ref,
    base_ref,
    slot_ref,
    dest_ref,
    out_ref,
    cv,
    wraw,
    lift_v,
    outw_v,
    din_v,
    dmid_v,
    dout_v,
    dest_s,
    noise,
    halo_out,
    halo_in,
    lifted,
    wconv,
    feat,
    fout,
    ein,
    emid,
    eout,
    hid1,
    hid2,
    lat,
    cond,
    edge,
    listing,
    gx,
    piece,
    arrived,
    swap_out,
    swap_in,
    local_sem,
    send_sem,
    recv_sem,
):
    section = lax.axis_index("section")
    tile = lax.axis_index("tile")
    half_rows = out_ref.shape[2] // 2
    cells = out_ref.shape[3]
    channels = din_ref.shape[1]
    fields = out_ref.shape[1]
    flat = fields * half_rows
    cin = lift_ref.shape[0]
    octet = half_rows // 2
    first = pl.multiple_of(section * half_rows, half_rows)

    copies = [
        pltpu.make_async_copy(coarse_ref, cv, local_sem.at[0]),
        pltpu.make_async_copy(conv_ref, wraw, local_sem.at[1]),
        pltpu.make_async_copy(
            base_ref.at[:, :, pl.ds(first, half_rows), :], noise.at[0], local_sem.at[2]
        ),
        pltpu.make_async_copy(
            slot_ref.at[:, :, pl.ds(first, half_rows), :], noise.at[1], local_sem.at[3]
        ),
        pltpu.make_async_copy(lift_ref, lift_v, local_sem.at[4]),
        pltpu.make_async_copy(outw_ref, outw_v, local_sem.at[5]),
        pltpu.make_async_copy(din_ref, din_v, local_sem.at[6]),
        pltpu.make_async_copy(dmid_ref, dmid_v, local_sem.at[7]),
        pltpu.make_async_copy(dout_ref, dout_v, local_sem.at[8]),
        pltpu.make_async_copy(dest_ref, dest_s, local_sem.at[9]),
    ]
    for copy in copies:
        copy.start()

    ahead = [lax.rem(tile + o, tiles) for o in range(REACH)]
    behind = [lax.rem(tile + tiles - o, tiles) for o in range(REACH)]

    barrier = pltpu.get_barrier_semaphore()
    for o in range(REACH - 1, 0, -1):
        for other in (ahead[o], behind[o]):
            pl.semaphore_signal(barrier, inc=1, device_id={"tile": other}, device_id_type=MESH)
    pl.semaphore_signal(
        barrier, inc=1, device_id={"section": 1 - section}, device_id_type=MESH
    )

    copies[0].wait()
    top_half = section == 0
    last_row = cv[:, 2 * half_rows - 1, :].astype(F32)
    first_row = cv[:, 0, :].astype(F32)
    halo_out[...] = jnp.zeros(halo_out.shape, BF)
    halo_out[0:cin, :] = jnp.where(top_half, last_row, first_row).astype(BF)

    for copy in copies[4:]:
        copy.wait()
    lift_half = lift_v[...].astype(F32) * 0.5
    lift_bf = lift_half.T.astype(BF)
    wide = jnp.dot(lift_bf, spread(cin, cin * octet, False, octet), preferred_element_type=F32)
    lane = lax.broadcasted_iota(jnp.int32, wide.shape, 1) % octet
    own = cv[:, pl.ds(first, half_rows), :].astype(F32)
    own = jnp.concatenate(
        [
            own[:, :octet, :].reshape(cin * octet, cells),
            own[:, octet:, :].reshape(cin * octet, cells),
        ],
        axis=1,
    ).astype(BF)
    for r in range(octet):
        weight = jnp.where(lane == r, wide, 0.0).astype(BF)
        lifted[(r + 1) * channels : (r + 2) * channels, :] = silu_of_half(
            jnp.dot(weight, own, preferred_element_type=F32)
        )
    copies[1].wait()
    for a in range(3):
        for b in range(3):
            wconv[b * channels : (b + 1) * channels, a * channels : (a + 1) * channels] = (
                (wraw[a, b].astype(F32) * 0.5).T.astype(BF)
            )
    wide_reg = jnp.dot(
        spread(fields * octet, fields, True, octet), outw_v[...], preferred_element_type=F32
    )
    row_reg = lax.broadcasted_iota(jnp.int32, wide_reg.shape, 0) % octet
    for r in range(octet):
        fout[:, r * channels : (r + 1) * channels] = jnp.where(row_reg == r, wide_reg, 0.0).astype(
            BF
        )
    pl.semaphore_wait(barrier, 2 * (REACH - 1) + 1)
    halo_target = lax.rem(jnp.where(top_half, tile + 1, tile + tiles - 1), tiles)
    halo_copy = pltpu.make_async_remote_copy(
        src_ref=halo_out,
        dst_ref=halo_in,
        send_sem=send_sem.at[0],
        recv_sem=recv_sem.at[0],
        device_id={"tile": halo_target},
        device_id_type=MESH,
    )
    halo_copy.start()

    lane_row = lax.broadcasted_iota(jnp.int32, (8, cells), 1)
    listed = jnp.full((8, cells), -1.0, F32)
    count = jnp.int32(MEMB)
    for j in range(REACH):
        listed = jnp.where(lane_row == j, dest_s[0, j].astype(F32), listed)
        count = count + jnp.where(dest_s[0, j] >= 0, 1, 0)
    listing[0] = listed

    def send_ahead(buffer, bank):
        started = []
        for o in range(REACH - 1, 0, -1):
            copy = pltpu.make_async_remote_copy(
                src_ref=buffer.at[0],
                dst_ref=buffer.at[o],
                send_sem=send_sem.at[bank * REACH + o],
                recv_sem=recv_sem.at[bank * REACH + o],
                device_id={"tile": ahead[o]},
                device_id_type=MESH,
            )
            copy.start()
            started.append(copy)
        return started

    list_copies = send_ahead(listing, 2)

    row_below = cv[:, half_rows, :].astype(F32)
    row_above = cv[:, half_rows - 1, :].astype(F32)
    edges = jnp.concatenate(
        [
            jnp.where(top_half, 0.0, row_above),
            jnp.where(top_half, row_below, 0.0),
        ],
        axis=1,
    ).astype(BF)
    lifted_edges = silu_of_half(jnp.dot(lift_bf, edges, preferred_element_type=F32))
    lifted[:channels, :cells] = lifted_edges[:, :cells]
    lifted[:channels, cells:] = lifted[octet * channels : (octet + 1) * channels, :cells]
    lifted[(octet + 1) * channels :, :cells] = lifted[channels : 2 * channels, cells:]
    lifted[(octet + 1) * channels :, cells:] = lifted_edges[:, cells:]
    column = lax.broadcasted_iota(jnp.int32, (channels, cells), 1)

    def combine(taps):
        left = pltpu.roll(taps[:channels], 1, 1)
        right = pltpu.roll(taps[2 * channels :], cells - 1, 1)
        return silu_of_half(
            taps[channels : 2 * channels]
            + jnp.where(column == 0, 0.0, left)
            + jnp.where(column == cells - 1, 0.0, right)
        )

    for r in range(octet):
        taps = jnp.dot(
            wconv[...],
            lifted[r * channels : (r + 3) * channels, :],
            preferred_element_type=F32,
        )
        for side in range(2):
            span = slice(side * cells, (side + 1) * cells)
            feat[r * channels : (r + 1) * channels, span] = combine(taps[:, span])
    produced = jnp.dot(fout[...], feat[...], preferred_element_type=F32)
    cond[0] = jnp.concatenate(
        [
            produced[c * octet : (c + 1) * octet, side * cells : (side + 1) * cells]
            for c in range(fields)
            for side in range(2)
        ],
        axis=0,
    ).astype(BF)

    cond_copies = send_ahead(cond, 1)
    halo_copy.wait_recv()
    inside = jnp.where(top_half, tile > 0, tile < tiles - 1)
    from_neighbour = jnp.where(inside, halo_in[0:cin, :].astype(F32), 0.0).astype(BF)
    halo = silu_of_half(jnp.dot(lift_bf, from_neighbour, preferred_element_type=F32))

    def rows_at(low, high):
        upper = lifted[low * channels : (low + 1) * channels, :cells]
        lower = lifted[high * channels : (high + 1) * channels, cells:]
        return jnp.where(top_half, upper, lower)

    around = jnp.concatenate(
        [
            jnp.where(top_half, halo, lifted[(octet - 1) * channels : octet * channels, cells:]),
            rows_at(1, octet),
            jnp.where(top_half, lifted[2 * channels : 3 * channels, :cells], halo),
        ],
        axis=0,
    )
    beside = combine(jnp.dot(wconv[...], around, preferred_element_type=F32))
    edge[0, :fields, :] = (
        jnp.dot(outw_v[...], beside, preferred_element_type=F32).astype(BF).astype(F32)
    )
    edge[0, fields:, :] = jnp.zeros((edge.shape[1] - fields, cells), F32)
    edge_copies = send_ahead(edge, 3)

    row_of = lax.broadcasted_iota(jnp.int32, (flat, cells), 0) % half_rows
    edge_row = jnp.where(top_half, 0, half_rows - 1)

    def with_edge(most, row):
        repeated = jnp.concatenate(
            [jnp.broadcast_to(row[c : c + 1, :], (half_rows, cells)) for c in range(fields)], axis=0
        )
        return jnp.where(row_of == edge_row, repeated, most)

    condition = with_edge(cond[0].astype(F32), edge[0]).astype(BF)

    wide_in = (
        jnp.dot(
            din_v[...].astype(F32).T.astype(BF),
            spread(2 * fields, 2 * flat, False, half_rows),
            preferred_element_type=F32,
        )
        * 0.5
    )
    lane_in = lax.broadcasted_iota(jnp.int32, wide_in.shape, 1) % half_rows
    wide_out = jnp.dot(
        spread(flat, fields, True, half_rows), dout_v[...], preferred_element_type=F32
    )
    row_out = lax.broadcasted_iota(jnp.int32, wide_out.shape, 0) % half_rows
    for r in range(half_rows):
        block = slice(r * channels, (r + 1) * channels)
        ein[block, :] = jnp.where(lane_in == r, wide_in, 0.0).astype(BF)
        eout[:, block] = jnp.where(row_out == r, wide_out, 0.0).astype(BF)
    mid = (dmid_v[...].astype(F32) * 0.5).astype(BF)
    emid[...] = jnp.zeros(emid.shape, BF)
    emid[:channels, :channels] = mid
    emid[channels:, channels:] = mid
    for k in range(2):
        copies[2 + k].wait()
        for m in range(MEMB):
            lat[k, :, m * cells : (m + 1) * cells] = (
                noise[k, m].astype(F32).reshape(flat, cells) * SIGMAS[0]
            )

    def denoise_step(group, position):
        latent = lat[group]
        stacked = jnp.concatenate([(latent * pick(position, 0)).astype(BF), gx[group]], axis=0)
        piece_rows = 4 * channels
        for r in range(half_rows // 4):
            block = slice(r * piece_rows, (r + 1) * piece_rows)
            hid1[block, :] = silu_of_half(
                jnp.dot(ein[block, :], stacked, preferred_element_type=F32)
            )
        for r in range(half_rows // 2):
            block = slice(2 * r * channels, 2 * (r + 1) * channels)
            hid2[block, :] = silu_of_half(
                jnp.dot(emid[...], hid1[block, :], preferred_element_type=F32)
            )
        found = jnp.dot(eout[...], hid2[...], preferred_element_type=F32)
        lat[group] = latent * pick(position, 1) + found * pick(position, 2)

    def run_steps(group, low, high):
        def step(position, carry):
            denoise_step(group, position)
            return carry

        lax.fori_loop(low, high, step, 0)

    gx[0] = jnp.concatenate([condition] * MEMB, axis=1)
    run_steps(0, 0, 5)

    for copy in list_copies:
        copy.wait_recv()
    me = tile.astype(F32)
    named = [
        jnp.max(jnp.where(listing[o] == me, 1.0, 0.0)) for o in range(REACH)
    ]
    chosen = []
    for o in range(REACH):
        rank = jnp.float32(0.0)
        for other in range(REACH):
            if other != o:
                rank = rank + jnp.where(behind[other] < behind[o], named[other], 0.0)
        chosen.append([jnp.where(rank == k, named[o], 0.0) for k in range(SLOTS)])
    for copy in cond_copies + edge_copies:
        copy.wait_recv()
    for k in range(SLOTS):
        served = cond[0].astype(F32) * chosen[0][k]
        served_row = edge[0] * chosen[0][k]
        for o in range(1, REACH):
            served = served + cond[o].astype(F32) * chosen[o][k]
            served_row = served_row + edge[o] * chosen[o][k]
        gx[1, :, k * cells : (k + 1) * cells] = with_edge(served, served_row).astype(BF)
    run_steps(1, 0, NSTEP)

    extra = lat[1] + gx[1].astype(F32)
    own_sample = None
    piece_copies = []
    for o in range(REACH - 1, -1, -1):
        sample = extra[:, :cells] * chosen[o][0]
        for k in range(1, SLOTS):
            sample = sample + extra[:, k * cells : (k + 1) * cells] * chosen[o][k]
        if o == 0:
            own_sample = sample
            continue
        piece[o] = sample.astype(BF)
        copy = pltpu.make_async_remote_copy(
            src_ref=piece.at[o],
            dst_ref=arrived.at[o],
            send_sem=send_sem.at[4 * REACH + o],
            recv_sem=recv_sem.at[4 * REACH + o],
            device_id={"tile": behind[o]},
            device_id_type=MESH,
        )
        copy.start()
        piece_copies.append(copy)

    run_steps(0, 5, NSTEP)

    base = lat[0] + gx[0].astype(F32)
    total = own_sample
    square = total * total
    for m in range(MEMB):
        sample = base[:, m * cells : (m + 1) * cells]
        total = total + sample
        square = square + sample * sample
    for o in range(1, REACH):
        piece_copies[REACH - 1 - o].wait_recv()
        sample = arrived[o].astype(F32)
        total = total + sample
        square = square + sample * sample
    members = count.astype(F32)
    mean = total / members
    variance = square / members - mean * mean

    swap_out[...] = jnp.where(top_half, variance, mean)
    swap = pltpu.make_async_remote_copy(
        src_ref=swap_out,
        dst_ref=swap_in,
        send_sem=send_sem.at[REACH],
        recv_sem=recv_sem.at[REACH],
        device_id={"section": 1 - section},
        device_id_type=MESH,
    )
    swap.start()
    kept = jnp.where(top_half, mean, variance)
    out_ref[0, :, pl.ds(first, half_rows), :] = kept.reshape(fields, half_rows, cells)
    halo_copy.wait_send()
    for copy in list_copies + cond_copies + edge_copies + piece_copies:
        copy.wait_send()
    swap.wait()
    second = pl.multiple_of((1 - section) * half_rows, half_rows)
    out_ref[0, :, pl.ds(second, half_rows), :] = swap_in[...].reshape(fields, half_rows, cells)


def body(tiles, *arrays):
    (coarse, lift, conv, outw, din, dmid, dout, base, slot, dest) = arrays
    cin, rows, cells = coarse.shape
    channels = lift.shape[0]
    lift = lift.T
    din = din.T
    fields = outw.shape[0]
    half = rows // 2
    flat = fields * half
    vmem = pl.BlockSpec(memory_space=pltpu.VMEM)
    in_hbm = pl.BlockSpec(memory_space=pltpu.HBM)
    scratch = [
        pltpu.VMEM(coarse.shape, BF),
        pltpu.VMEM(conv.shape, BF),
        pltpu.VMEM(lift.shape, BF),
        pltpu.VMEM(outw.shape, BF),
        pltpu.VMEM(din.shape, BF),
        pltpu.VMEM(dmid.shape, BF),
        pltpu.VMEM(dout.shape, BF),
        pltpu.SMEM(dest.shape, jnp.int32),
        pltpu.VMEM((2, MEMB, fields, half, cells), BF),
        pltpu.VMEM((16, cells), BF),
        pltpu.VMEM((16, cells), BF),
        pltpu.VMEM(((half // 2 + 2) * channels, 2 * cells), BF),
        pltpu.VMEM((3 * channels, 3 * channels), BF),
        pltpu.VMEM((half // 2 * channels, 2 * cells), BF),
        pltpu.VMEM((fields * half // 2, half // 2 * channels), BF),
        pltpu.VMEM((half * channels, 2 * flat), BF),
        pltpu.VMEM((2 * channels, 2 * channels), BF),
        pltpu.VMEM((flat, half * channels), BF),
        pltpu.VMEM((half * channels, MEMB * cells), BF),
        pltpu.VMEM((half * channels, MEMB * cells), BF),
        pltpu.VMEM((2, flat, MEMB * cells), F32),
        pltpu.VMEM((REACH, flat, cells), BF),
        pltpu.VMEM((REACH, 8, cells), F32),
        pltpu.VMEM((REACH, 8, cells), F32),
        pltpu.VMEM((2, flat, MEMB * cells), BF),
        pltpu.VMEM((REACH, flat, cells), BF),
        pltpu.VMEM((REACH, flat, cells), BF),
        pltpu.VMEM((flat, cells), F32),
        pltpu.VMEM((flat, cells), F32),
        pltpu.SemaphoreType.DMA((10,)),
        pltpu.SemaphoreType.DMA((5 * REACH,)),
        pltpu.SemaphoreType.DMA((5 * REACH,)),
    ]
    return pl.pallas_call(
        functools.partial(kernel, tiles),
        out_shape=jax.ShapeDtypeStruct((1, fields, rows, cells), F32),
        in_specs=[in_hbm] * 10,
        out_specs=vmem,
        scratch_shapes=scratch,
        compiler_params=pltpu.CompilerParams(
            collective_id=0, has_side_effects=True, vmem_limit_bytes=48 * 2**20
        ),
        name="ensemble",
    )(
        *[
            pltpu.with_memory_space_constraint(array, pltpu.HBM)
            for array in (coarse, lift, conv, outw, din, dmid, dout, base, slot, dest)
        ]
    )


def solution(mesh):
    in_specs = (
        P(None, "tile", None),
        P(),
        P(),
        P(),
        P(),
        P(),
        P(),
        P(None, None, "tile", None),
        P(None, None, "tile", None),
        P("tile", None),
    )
    out_specs = P("section", None, "tile", None)
    return jax.shard_map(
        functools.partial(body, mesh.shape["tile"]),
        mesh=mesh,
        in_specs=in_specs,
        out_specs=out_specs,
        check_vma=False,
    )
```

```python
import functools
import math

import jax
import jax.numpy as jnp
from jax import lax
from jax.experimental import pallas as pl
from jax.experimental.pallas import tpu as pltpu
from jax.sharding import PartitionSpec as P

MESH = pl.DeviceIdType.MESH
BF = jnp.bfloat16
F32 = jnp.float32
MEMB = 4
SLOTS = 4
NSTEP = 6
REACH = 8
SIGMA_MAX = 4.0
SIGMA_MIN = 0.25
PLAN_POWER = 7.0


def sigma_table(step_count):
    upper_root = SIGMA_MAX ** (1.0 / PLAN_POWER)
    lower_root = SIGMA_MIN ** (1.0 / PLAN_POWER)
    values = []
    for position in range(step_count):
        fraction = position / (step_count - 1)
        values.append((upper_root + fraction * (lower_root - upper_root)) ** PLAN_POWER)
    values.append(0.0)
    return values


SIGMAS = sigma_table(NSTEP)


def step_factors():
    table = []
    for position in range(NSTEP):
        now, later = SIGMAS[position], SIGMAS[position + 1]
        scale = 1.0 / math.sqrt(now * now + 1.0)
        slope = (later - now) / now
        table.append((scale, 1.0 + slope * (1.0 - scale * scale), -slope * now * scale))
    return table


FACTORS = step_factors()


def pick(position, column):
    value = jnp.float32(FACTORS[NSTEP - 1][column])
    for step in range(NSTEP - 2, -1, -1):
        value = jnp.where(position == step, jnp.float32(FACTORS[step][column]), value)
    return value


def silu_of_half(half):
    return (half + half * jnp.tanh(half)).astype(BF)


def spread(rows, columns, by_row, group):
    i = lax.broadcasted_iota(jnp.int32, (rows, columns), 0)
    j = lax.broadcasted_iota(jnp.int32, (rows, columns), 1)
    same = (i // group == j) if by_row else (j // group == i)
    return same.astype(F32).astype(BF)


def kernel(
    tiles,
    coarse_ref,
    lift_ref,
    conv_ref,
    outw_ref,
    din_ref,
    dmid_ref,
    dout_ref,
    base_ref,
    slot_ref,
    dest_ref,
    out_ref,
    cv,
    wraw,
    lift_v,
    outw_v,
    din_v,
    dmid_v,
    dout_v,
    dest_s,
    noise,
    halo_out,
    halo_in,
    lifted,
    wconv,
    feat,
    fout,
    ein,
    emid,
    eout,
    hid1,
    hid2,
    lat,
    cond,
    edge,
    listing,
    gx,
    piece,
    arrived,
    swap_out,
    swap_in,
    local_sem,
    send_sem,
    recv_sem,
):
    section = lax.axis_index("section")
    tile = lax.axis_index("tile")
    half_rows = out_ref.shape[2] // 2
    cells = out_ref.shape[3]
    channels = din_ref.shape[1]
    fields = out_ref.shape[1]
    flat = fields * half_rows
    cin = lift_ref.shape[0]
    octet = half_rows // 2
    first = pl.multiple_of(section * half_rows, half_rows)

    copies = [
        pltpu.make_async_copy(coarse_ref, cv, local_sem.at[0]),
        pltpu.make_async_copy(conv_ref, wraw, local_sem.at[1]),
        pltpu.make_async_copy(
            base_ref.at[:, :, pl.ds(first, half_rows), :], noise.at[0], local_sem.at[2]
        ),
        pltpu.make_async_copy(
            slot_ref.at[:, :, pl.ds(first, half_rows), :], noise.at[1], local_sem.at[3]
        ),
        pltpu.make_async_copy(lift_ref, lift_v, local_sem.at[4]),
        pltpu.make_async_copy(outw_ref, outw_v, local_sem.at[5]),
        pltpu.make_async_copy(din_ref, din_v, local_sem.at[6]),
        pltpu.make_async_copy(dmid_ref, dmid_v, local_sem.at[7]),
        pltpu.make_async_copy(dout_ref, dout_v, local_sem.at[8]),
        pltpu.make_async_copy(dest_ref, dest_s, local_sem.at[9]),
    ]
    for copy in copies:
        copy.start()

    ahead = [lax.rem(tile + o, tiles) for o in range(REACH)]
    behind = [lax.rem(tile + tiles - o, tiles) for o in range(REACH)]

    barrier = pltpu.get_barrier_semaphore()
    for o in range(REACH - 1, 0, -1):
        for other in (ahead[o], behind[o]):
            pl.semaphore_signal(barrier, inc=1, device_id={"tile": other}, device_id_type=MESH)
    pl.semaphore_signal(
        barrier, inc=1, device_id={"section": 1 - section}, device_id_type=MESH
    )

    copies[0].wait()
    top_half = section == 0
    last_row = cv[:, 2 * half_rows - 1, :].astype(F32)
    first_row = cv[:, 0, :].astype(F32)
    halo_out[...] = jnp.zeros(halo_out.shape, BF)
    halo_out[0:cin, :] = jnp.where(top_half, last_row, first_row).astype(BF)

    for copy in copies[4:]:
        copy.wait()
    lift_half = lift_v[...].astype(F32) * 0.5
    lift_bf = lift_half.T.astype(BF)
    wide = jnp.dot(lift_bf, spread(cin, cin * octet, False, octet), preferred_element_type=F32)
    lane = lax.broadcasted_iota(jnp.int32, wide.shape, 1) % octet
    own = cv[:, pl.ds(first, half_rows), :].astype(F32)
    own = jnp.concatenate(
        [
            own[:, :octet, :].reshape(cin * octet, cells),
            own[:, octet:, :].reshape(cin * octet, cells),
        ],
        axis=1,
    ).astype(BF)
    for r in range(octet):
        weight = jnp.where(lane == r, wide, 0.0).astype(BF)
        lifted[(r + 1) * channels : (r + 2) * channels, :] = silu_of_half(
            jnp.dot(weight, own, preferred_element_type=F32)
        )
    copies[1].wait()
    for a in range(3):
        for b in range(3):
            wconv[b * channels : (b + 1) * channels, a * channels : (a + 1) * channels] = (
                (wraw[a, b].astype(F32) * 0.5).T.astype(BF)
            )
    wide_reg = jnp.dot(
        spread(fields * octet, fields, True, octet), outw_v[...], preferred_element_type=F32
    )
    row_reg = lax.broadcasted_iota(jnp.int32, wide_reg.shape, 0) % octet
    for r in range(octet):
        fout[:, r * channels : (r + 1) * channels] = jnp.where(row_reg == r, wide_reg, 0.0).astype(
            BF
        )
    pl.semaphore_wait(barrier, 2 * (REACH - 1) + 1)
    halo_target = lax.rem(jnp.where(top_half, tile + 1, tile + tiles - 1), tiles)
    halo_copy = pltpu.make_async_remote_copy(
        src_ref=halo_out,
        dst_ref=halo_in,
        send_sem=send_sem.at[0],
        recv_sem=recv_sem.at[0],
        device_id={"tile": halo_target},
        device_id_type=MESH,
    )
    halo_copy.start()

    lane_row = lax.broadcasted_iota(jnp.int32, (8, cells), 1)
    listed = jnp.full((8, cells), -1.0, F32)
    count = jnp.int32(MEMB)
    for j in range(REACH):
        listed = jnp.where(lane_row == j, dest_s[0, j].astype(F32), listed)
        count = count + jnp.where(dest_s[0, j] >= 0, 1, 0)
    listing[0] = listed

    def send_ahead(buffer, bank):
        started = []
        for o in range(REACH - 1, 0, -1):
            copy = pltpu.make_async_remote_copy(
                src_ref=buffer.at[0],
                dst_ref=buffer.at[o],
                send_sem=send_sem.at[bank * REACH + o],
                recv_sem=recv_sem.at[bank * REACH + o],
                device_id={"tile": ahead[o]},
                device_id_type=MESH,
            )
            copy.start()
            started.append(copy)
        return started

    list_copies = send_ahead(listing, 2)

    row_below = cv[:, half_rows, :].astype(F32)
    row_above = cv[:, half_rows - 1, :].astype(F32)
    edges = jnp.concatenate(
        [
            jnp.where(top_half, 0.0, row_above),
            jnp.where(top_half, row_below, 0.0),
        ],
        axis=1,
    ).astype(BF)
    lifted_edges = silu_of_half(jnp.dot(lift_bf, edges, preferred_element_type=F32))
    lifted[:channels, :cells] = lifted_edges[:, :cells]
    lifted[:channels, cells:] = lifted[octet * channels : (octet + 1) * channels, :cells]
    lifted[(octet + 1) * channels :, :cells] = lifted[channels : 2 * channels, cells:]
    lifted[(octet + 1) * channels :, cells:] = lifted_edges[:, cells:]
    column = lax.broadcasted_iota(jnp.int32, (channels, cells), 1)

    def combine(taps):
        left = pltpu.roll(taps[:channels], 1, 1)
        right = pltpu.roll(taps[2 * channels :], cells - 1, 1)
        return silu_of_half(
            taps[channels : 2 * channels]
            + jnp.where(column == 0, 0.0, left)
            + jnp.where(column == cells - 1, 0.0, right)
        )

    for r in range(octet):
        taps = jnp.dot(
            wconv[...],
            lifted[r * channels : (r + 3) * channels, :],
            preferred_element_type=F32,
        )
        for side in range(2):
            span = slice(side * cells, (side + 1) * cells)
            feat[r * channels : (r + 1) * channels, span] = combine(taps[:, span])
    produced = jnp.dot(fout[...], feat[...], preferred_element_type=F32)
    cond[0] = jnp.concatenate(
        [
            produced[c * octet : (c + 1) * octet, side * cells : (side + 1) * cells]
            for c in range(fields)
            for side in range(2)
        ],
        axis=0,
    ).astype(BF)

    cond_copies = send_ahead(cond, 1)
    halo_copy.wait_recv()
    inside = jnp.where(top_half, tile > 0, tile < tiles - 1)
    from_neighbour = jnp.where(inside, halo_in[0:cin, :].astype(F32), 0.0).astype(BF)
    halo = silu_of_half(jnp.dot(lift_bf, from_neighbour, preferred_element_type=F32))

    def rows_at(low, high):
        upper = lifted[low * channels : (low + 1) * channels, :cells]
        lower = lifted[high * channels : (high + 1) * channels, cells:]
        return jnp.where(top_half, upper, lower)

    around = jnp.concatenate(
        [
            jnp.where(top_half, halo, lifted[(octet - 1) * channels : octet * channels, cells:]),
            rows_at(1, octet),
            jnp.where(top_half, lifted[2 * channels : 3 * channels, :cells], halo),
        ],
        axis=0,
    )
    beside = combine(jnp.dot(wconv[...], around, preferred_element_type=F32))
    edge[0, :fields, :] = (
        jnp.dot(outw_v[...], beside, preferred_element_type=F32).astype(BF).astype(F32)
    )
    edge[0, fields:, :] = jnp.zeros((edge.shape[1] - fields, cells), F32)
    edge_copies = send_ahead(edge, 3)

    row_of = lax.broadcasted_iota(jnp.int32, (flat, cells), 0) % half_rows
    edge_row = jnp.where(top_half, 0, half_rows - 1)

    def with_edge(most, row):
        repeated = jnp.concatenate(
            [jnp.broadcast_to(row[c : c + 1, :], (half_rows, cells)) for c in range(fields)], axis=0
        )
        return jnp.where(row_of == edge_row, repeated, most)

    condition = with_edge(cond[0].astype(F32), edge[0]).astype(BF)

    wide_in = (
        jnp.dot(
            din_v[...].astype(F32).T.astype(BF),
            spread(2 * fields, 2 * flat, False, half_rows),
            preferred_element_type=F32,
        )
        * 0.5
    )
    lane_in = lax.broadcasted_iota(jnp.int32, wide_in.shape, 1) % half_rows
    wide_out = jnp.dot(
        spread(fields * octet, fields, True, octet), dout_v[...], preferred_element_type=F32
    )
    row_out = lax.broadcasted_iota(jnp.int32, wide_out.shape, 0) % octet
    for r in range(half_rows):
        block = slice(r * channels, (r + 1) * channels)
        ein[block, :] = jnp.where(lane_in == r, wide_in, 0.0).astype(BF)
        if r < octet:
            eout[:, block] = jnp.where(row_out == r, wide_out, 0.0).astype(BF)
    mid = (dmid_v[...].astype(F32) * 0.5).astype(BF)
    emid[...] = jnp.zeros(emid.shape, BF)
    emid[:channels, :channels] = mid
    emid[channels:, channels:] = mid
    for k in range(2):
        copies[2 + k].wait()
        for m in range(MEMB):
            lat[k, :, m * cells : (m + 1) * cells] = (
                noise[k, m].astype(F32).reshape(flat, cells) * SIGMAS[0]
            )

    def denoise_step(group, position):
        latent = lat[group]
        stacked = jnp.concatenate([(latent * pick(position, 0)).astype(BF), gx[group]], axis=0)
        piece_rows = 4 * channels
        for r in range(half_rows // 4):
            block = slice(r * piece_rows, (r + 1) * piece_rows)
            hid1[block, :] = silu_of_half(
                jnp.dot(ein[block, :], stacked, preferred_element_type=F32)
            )
        for r in range(half_rows // 2):
            block = slice(2 * r * channels, 2 * (r + 1) * channels)
            hid2[block, :] = silu_of_half(
                jnp.dot(emid[...], hid1[block, :], preferred_element_type=F32)
            )
        span = octet * channels
        parts = [
            jnp.dot(
                eout[:, :span],
                hid2[side * span : (side + 1) * span, :],
                preferred_element_type=F32,
            )
            for side in range(2)
        ]
        found = jnp.concatenate(
            [
                parts[side][c * octet : (c + 1) * octet]
                for c in range(fields)
                for side in range(2)
            ],
            axis=0,
        )
        lat[group] = latent * pick(position, 1) + found * pick(position, 2)

    def run_steps(group, low, high):
        def step(position, carry):
            denoise_step(group, position)
            return carry

        lax.fori_loop(low, high, step, 0)

    gx[0] = jnp.concatenate([condition] * MEMB, axis=1)
    run_steps(0, 0, 5)

    for copy in list_copies:
        copy.wait_recv()
    me = tile.astype(F32)
    named = [
        jnp.max(jnp.where(listing[o] == me, 1.0, 0.0)) for o in range(REACH)
    ]
    chosen = []
    for o in range(REACH):
        rank = jnp.float32(0.0)
        for other in range(REACH):
            if other != o:
                rank = rank + jnp.where(behind[other] < behind[o], named[other], 0.0)
        chosen.append([jnp.where(rank == k, named[o], 0.0) for k in range(SLOTS)])
    for copy in cond_copies + edge_copies:
        copy.wait_recv()
    for k in range(SLOTS):
        served = cond[0].astype(F32) * chosen[0][k]
        served_row = edge[0] * chosen[0][k]
        for o in range(1, REACH):
            served = served + cond[o].astype(F32) * chosen[o][k]
            served_row = served_row + edge[o] * chosen[o][k]
        gx[1, :, k * cells : (k + 1) * cells] = with_edge(served, served_row).astype(BF)
    run_steps(1, 0, NSTEP)

    extra = lat[1] + gx[1].astype(F32)
    own_sample = None
    piece_copies = []
    for o in range(REACH - 1, -1, -1):
        sample = extra[:, :cells] * chosen[o][0]
        for k in range(1, SLOTS):
            sample = sample + extra[:, k * cells : (k + 1) * cells] * chosen[o][k]
        if o == 0:
            own_sample = sample
            continue
        piece[o] = sample.astype(BF)
        copy = pltpu.make_async_remote_copy(
            src_ref=piece.at[o],
            dst_ref=arrived.at[o],
            send_sem=send_sem.at[4 * REACH + o],
            recv_sem=recv_sem.at[4 * REACH + o],
            device_id={"tile": behind[o]},
            device_id_type=MESH,
        )
        copy.start()
        piece_copies.append(copy)

    run_steps(0, 5, NSTEP)

    base = lat[0] + gx[0].astype(F32)
    total = own_sample
    square = total * total
    for m in range(MEMB):
        sample = base[:, m * cells : (m + 1) * cells]
        total = total + sample
        square = square + sample * sample
    for o in range(1, REACH):
        piece_copies[REACH - 1 - o].wait_recv()
        sample = arrived[o].astype(F32)
        total = total + sample
        square = square + sample * sample
    members = count.astype(F32)
    mean = total / members
    variance = square / members - mean * mean

    swap_out[...] = jnp.where(top_half, variance, mean)
    swap = pltpu.make_async_remote_copy(
        src_ref=swap_out,
        dst_ref=swap_in,
        send_sem=send_sem.at[REACH],
        recv_sem=recv_sem.at[REACH],
        device_id={"section": 1 - section},
        device_id_type=MESH,
    )
    swap.start()
    kept = jnp.where(top_half, mean, variance)
    out_ref[0, :, pl.ds(first, half_rows), :] = kept.reshape(fields, half_rows, cells)
    halo_copy.wait_send()
    for copy in list_copies + cond_copies + edge_copies + piece_copies:
        copy.wait_send()
    swap.wait()
    second = pl.multiple_of((1 - section) * half_rows, half_rows)
    out_ref[0, :, pl.ds(second, half_rows), :] = swap_in[...].reshape(fields, half_rows, cells)


def body(tiles, *arrays):
    (coarse, lift, conv, outw, din, dmid, dout, base, slot, dest) = arrays
    cin, rows, cells = coarse.shape
    channels = lift.shape[0]
    lift = lift.T
    din = din.T
    fields = outw.shape[0]
    half = rows // 2
    flat = fields * half
    vmem = pl.BlockSpec(memory_space=pltpu.VMEM)
    in_hbm = pl.BlockSpec(memory_space=pltpu.HBM)
    scratch = [
        pltpu.VMEM(coarse.shape, BF),
        pltpu.VMEM(conv.shape, BF),
        pltpu.VMEM(lift.shape, BF),
        pltpu.VMEM(outw.shape, BF),
        pltpu.VMEM(din.shape, BF),
        pltpu.VMEM(dmid.shape, BF),
        pltpu.VMEM(dout.shape, BF),
        pltpu.SMEM(dest.shape, jnp.int32),
        pltpu.VMEM((2, MEMB, fields, half, cells), BF),
        pltpu.VMEM((16, cells), BF),
        pltpu.VMEM((16, cells), BF),
        pltpu.VMEM(((half // 2 + 2) * channels, 2 * cells), BF),
        pltpu.VMEM((3 * channels, 3 * channels), BF),
        pltpu.VMEM((half // 2 * channels, 2 * cells), BF),
        pltpu.VMEM((fields * half // 2, half // 2 * channels), BF),
        pltpu.VMEM((half * channels, 2 * flat), BF),
        pltpu.VMEM((2 * channels, 2 * channels), BF),
        pltpu.VMEM((flat // 2, half // 2 * channels), BF),
        pltpu.VMEM((half * channels, MEMB * cells), BF),
        pltpu.VMEM((half * channels, MEMB * cells), BF),
        pltpu.VMEM((2, flat, MEMB * cells), F32),
        pltpu.VMEM((REACH, flat, cells), BF),
        pltpu.VMEM((REACH, 8, cells), F32),
        pltpu.VMEM((REACH, 8, cells), F32),
        pltpu.VMEM((2, flat, MEMB * cells), BF),
        pltpu.VMEM((REACH, flat, cells), BF),
        pltpu.VMEM((REACH, flat, cells), BF),
        pltpu.VMEM((flat, cells), F32),
        pltpu.VMEM((flat, cells), F32),
        pltpu.SemaphoreType.DMA((10,)),
        pltpu.SemaphoreType.DMA((5 * REACH,)),
        pltpu.SemaphoreType.DMA((5 * REACH,)),
    ]
    return pl.pallas_call(
        functools.partial(kernel, tiles),
        out_shape=jax.ShapeDtypeStruct((1, fields, rows, cells), F32),
        in_specs=[in_hbm] * 10,
        out_specs=vmem,
        scratch_shapes=scratch,
        compiler_params=pltpu.CompilerParams(
            collective_id=0, has_side_effects=True, vmem_limit_bytes=48 * 2**20
        ),
        name="ensemble",
    )(
        *[
            pltpu.with_memory_space_constraint(array, pltpu.HBM)
            for array in (coarse, lift, conv, outw, din, dmid, dout, base, slot, dest)
        ]
    )


def solution(mesh):
    in_specs = (
        P(None, "tile", None),
        P(),
        P(),
        P(),
        P(),
        P(),
        P(),
        P(None, None, "tile", None),
        P(None, None, "tile", None),
        P("tile", None),
    )
    out_specs = P("section", None, "tile", None)
    return jax.shard_map(
        functools.partial(body, mesh.shape["tile"]),
        mesh=mesh,
        in_specs=in_specs,
        out_specs=out_specs,
        check_vma=False,
    )
```
